32 devices in a mesh: seq: 8 (over y, x, core), exp: 4 (over z).
Axes of the slice: x: 2, y: 2, z: 4, core: 2. Of those that a mesh axis runs over, the one named last changes fastest.
Arguments:
- queries: bfloat16 [1024, 4096], P('seq', 'exp'), may hold values from -135 to 135
- attn_keys: bfloat16 [1024, 512], P('seq', 'exp'), may hold values from -4.5 to 4.5
- attn_values: bfloat16 [1024, 512], P('seq', 'exp'), may hold values from -6 to 6
- sink_logits: float32 [64], P('exp'), may hold values from -1 to 3
- out_proj: bfloat16 [4096, 2880], P('exp'), may hold values from -0.09375 to 0.09375
- residual: bfloat16 [1024, 2880], P('seq', 'exp'), may hold values from -6 to 6
- norm_gain: float32 [2880], replicated, may hold values from 0.5 to 1.5
- doc_start: int32 [1024], P('seq'), may hold values from 0 to 1023, as said below
- expert_ids: int32 [1024, 4], P('seq'), may hold values from 0 to 7, all different within a row; in each aligned block of 128 rows (0 to 127, 128 to 255, ...) at most 128 rows name the same one
- route_scores: float32 [1024, 4], P('seq'), may hold values from 0.2 to 1
- w_gate_up: bfloat16 [8, 2, 2880, 2880], P('seq', None, None, 'exp'), may hold values from -0.109375 to 0.109375
- w_down: bfloat16 [8, 2880, 2880], P('seq', 'exp'), may hold values from -0.109375 to 0.109375
- control: float32 [2880], replicated, may hold values from 0 to 1
Outputs:
- grad_gate_up: bfloat16 [8, 2, 2880, 2880], P('seq', None, None, 'exp')
The draws below stay inside these ranges and needn't reach their ends.
Inputs may be any that keep to these rules, and one draw needn't show every extreme that they name: `expert_ids`: each row names 4 different experts; among the 128 rows of one index of seq no expert is named by more than 128 rows, a bound that some block reaches. doc_start of a position is the first position of its document: never above the position itself, never falling along the pack, equal within a document; position 0 starts a document, and the last position of the pack is a document of its own.
All inputs are finite; a program needn't handle non-finite values.
Results may differ from the reference program's by a relative error of at most 0.0075.
Values may be sent and summed in bfloat16 or wider, within the bound.
A program may use at most 128 MiB of HBM per device.

```python
import math
import jax
import jax.numpy as jnp
import numpy as np
from jax import lax

D = 2880
HEADS = 64
KV_HEADS = 8
HEAD_DIM = 64
FF = 2880
WINDOW = 128
TOPK = 4
SEG = 128
PACK = 1024
EXPERTS = 8
CAP = 128
HID_BLOCKS = 4
N_SEQ = 8


def paired_rows(key):
    base = jax.random.fold_in(key, 11)
    key_keys, key_queries = jax.random.split(base, 2)
    key_rows = jnp.clip(jax.random.normal(key_keys, (PACK, KV_HEADS * HEAD_DIM), jnp.float32), -4.5, 4.5)
    query_rows = jnp.clip(jax.random.normal(key_queries, (PACK, HEADS * HEAD_DIM), jnp.float32), -4.5, 4.5)
    return (query_rows, key_rows)


def draw_queries(key, part):
    return paired_rows(key)[0].astype(jnp.bfloat16)


def draw_attn_keys(key, part):
    return paired_rows(key)[1].astype(jnp.bfloat16)


def draw_doc_start(key, part):
    folded = jax.random.fold_in(key, 23)
    position = jnp.arange(PACK, dtype=jnp.int32)
    cuts = (jax.random.randint(folded, (PACK,), 0, 2 * SEG) == 0) | (position == 0) | (position == PACK - 1)
    return lax.cummax(jnp.where(cuts, position, 0), axis=0)


def steps_of(key, shape, pieces, smallest, high):
    gain = 1.0
    for axis_at, shards_of in pieces:
        steps = jax.random.uniform(jax.random.fold_in(jax.random.fold_in(key, 6), axis_at), (shards_of,), jnp.float32, smallest / len(pieces), high / len(pieces))
        gain = gain * jnp.repeat(jnp.exp(steps), shape[axis_at] // shards_of).reshape((-1,) + (1,) * (len(shape) - 1 - axis_at))
    return gain


def assign_block(rng, own, number, rows, count, top, reach, slope):
    ranking = jax.random.permutation(rng, count)
    packed, common = shares(count, rows * top, reach, slope, True), shares(count, rows * top, reach, slope, False)
    places = jnp.arange(count)

    def named(lengths, rotation):
        used = int((lengths > 0).sum())
        fixed = max(1, used // 4)
        moved = fixed + (places - fixed + rotation * (used - fixed)) % max(1, count - fixed)
        return jnp.zeros((count,), jnp.int32).at[ranking[jnp.where(places < fixed, places, moved)]].set(jnp.asarray(lengths, jnp.int32))

    lengths = jnp.where(number % 4 == 0, named(packed, number // 4), named(common, number - number // 4 - 1))
    mixed = jax.random.permutation(jax.random.fold_in(own, 3), count)
    source_of, sink = mixed[0:count // 2 * 2:2], mixed[1:count // 2 * 2:2]
    margin = jnp.minimum(lengths[source_of] - 1, reach - lengths[sink]) // 2
    margin = jnp.where((source_of == ranking[0]) | (sink == ranking[0]) | (lengths[sink] == 0), 0, jnp.maximum(margin, 0))
    moved = jax.random.randint(jax.random.fold_in(own, 4), (count // 2,), 0, 1 << 20) % (margin + 1)
    lengths = lengths.at[source_of].add(-moved).at[sink].add(moved)
    items = jnp.searchsorted(jnp.cumsum(lengths), jnp.arange(rows * top), side="right").astype(jnp.int32)
    grid = items.reshape(top, rows).T
    grid = grid[jax.random.permutation(jax.random.fold_in(own, 1), rows)]
    rotation = jax.random.randint(jax.random.fold_in(own, 2), (rows, 1), 0, top)
    return jnp.take_along_axis(grid, (jnp.arange(top)[None, :] + rotation) % top, axis=1)


def shares(number_of, total, reach, skew, full):
    portions = [(1 << 20) // math.isqrt(standing ** skew) + 1 for standing in range(1, number_of + 1)]
    largest = reach if full else min(reach, max(-(-total // number_of), total * portions[0] // sum(portions)))
    least = 1 if total - largest >= number_of - 1 else 0
    holding, spare = [largest] + [least] * (number_of - 1), total - largest - least * (number_of - 1)
    while spare > 0:
        movable = [i for i in range(1, number_of) if holding[i] < largest] or [i for i in range(1, number_of) if holding[i] < reach]
        mass, budget = sum([portions[i] for i in movable]), spare
        for i in movable:
            extra = min(reach - holding[i], max(1, budget * portions[i] // mass), spare)
            holding[i] = holding[i] + extra
            spare = spare - extra
    return np.array(holding)


def scatter_about(stream_key, dims, deviation, most, pieces=(), kind=jnp.bfloat16):
    gain = steps_of(stream_key, dims, pieces, -0.22, 0.18) if pieces else 1.0
    array = jax.random.normal(stream_key, dims, jnp.float32) * deviation * gain
    return jnp.minimum(jnp.maximum(array, -most), most).astype(kind)


def setup_inputs(seed: int = 0) -> dict:
    splits = jax.random.split(jax.random.key(seed), 14)
    queries = draw_queries(jax.random.fold_in(splits[13], 71), 0)
    attn_keys = draw_attn_keys(jax.random.fold_in(splits[13], 71), 0)
    attn_values = scatter_about(splits[2], (PACK, KV_HEADS * HEAD_DIM), 1.0, 6.0, ((0, 8), (1, 4)))
    sink_logits = jnp.clip(-1.0 + 4.0 * jax.random.uniform(splits[3], (HEADS,), jnp.float32) ** steps_of(splits[3], (HEADS,), ((0, 4),), -0.2, 0.2), -1.0, 3.0)
    out_proj = scatter_about(splits[4], (HEADS * HEAD_DIM, D), (HEADS * HEAD_DIM) ** -0.5, 0.09375, ((0, 4),))
    residual = scatter_about(splits[5], (PACK, D), 1.0, 6.0, ((0, 8), (1, 4)))
    norm_gain = jnp.clip(1.0 + 0.1 * jax.random.normal(splits[6], (D,), jnp.float32), 0.5, 1.5)
    doc_start = draw_doc_start(jax.random.fold_in(splits[13], 71), 0)
    expert_ids_keys = jax.random.split(jax.random.fold_in(splits[8], 1), PACK // SEG)
    expert_ids_turns = jax.random.permutation(jax.random.fold_in(splits[8], 3), PACK // SEG)
    expert_ids = jax.vmap(lambda own, number: assign_block(jax.random.fold_in(splits[8], 2), own, number, SEG, EXPERTS, TOPK, CAP, 1))(expert_ids_keys, expert_ids_turns).reshape((PACK, TOPK))
    route_scores = jnp.clip(0.2 + 0.8 * jax.random.uniform(splits[9], (PACK, TOPK), jnp.float32) ** steps_of(splits[9], (PACK, TOPK), ((0, 8),), -0.2, 0.2), 0.2, 1.0)
    w_gate_up = scatter_about(splits[10], (EXPERTS, 2, D, FF), D ** -0.5, 0.109375, ((0, 8), (3, 4)))
    w_down = scatter_about(splits[11], (EXPERTS, FF, D), FF ** -0.5, 0.109375, ((0, 8), (1, 4)))
    control = jnp.clip(jax.random.uniform(splits[12], (D,), jnp.float32, 0.0, 1.0), 0.0, 1.0)
    return {"queries": queries, "attn_keys": attn_keys, "attn_values": attn_values, "sink_logits": sink_logits, "out_proj": out_proj, "residual": residual, "norm_gain": norm_gain, "doc_start": doc_start, "expert_ids": expert_ids, "route_scores": route_scores, "w_gate_up": w_gate_up, "w_down": w_down, "control": control}


GLU_ALPHA = 1.702
STEER = 6.5
EPSILON = 1e-05
MASKED = -1e+30

def attend(query_rows, keys_all, values_all, sink_logits, starts, query_pos, key_pos):
    group_size = HEADS // KV_HEADS
    allowed = (key_pos[None, :] <= query_pos[:, None]) & (key_pos[None, :] > query_pos[:, None] - WINDOW) & (key_pos[None, :] >= starts[:, None])
    grouped = query_rows.reshape(SEG, KV_HEADS, group_size, HEAD_DIM).astype(jnp.float32)
    keys_grid = keys_all.reshape(SEG + WINDOW, KV_HEADS, HEAD_DIM).astype(jnp.float32)
    values_grid = values_all.reshape(SEG + WINDOW, KV_HEADS, HEAD_DIM).astype(jnp.float32)
    scores = jnp.einsum('qcgd,kcd->cgqk', grouped, keys_grid) * HEAD_DIM ** (-0.5)
    masked_scores = jnp.where(allowed[None, None], scores, MASKED)
    sink_grid = sink_logits.reshape(KV_HEADS, group_size, 1, 1)
    row_top = jnp.maximum(lax.optimization_barrier(jnp.max(masked_scores, axis=-1, keepdims=True)), sink_grid)
    expo_scores = jnp.where(allowed[None, None], jnp.exp(masked_scores - row_top), 0.0)
    denominator = lax.optimization_barrier(jnp.sum(expo_scores, axis=-1, keepdims=True)) + jnp.exp(sink_grid - row_top)
    attn_weights = (expo_scores / denominator).astype(jnp.bfloat16)
    mixed_heads = jnp.einsum('cgqk,kcd->qcgd', attn_weights.astype(jnp.float32), values_grid)
    return mixed_heads.astype(jnp.bfloat16).reshape(SEG, HEADS * HEAD_DIM)

def reference(queries, attn_keys, attn_values, sink_logits, out_proj, residual, norm_gain, doc_start, expert_ids, route_scores, w_gate_up, w_down, control):
    zero_rim = jnp.zeros((WINDOW, KV_HEADS * HEAD_DIM), attn_keys.dtype)
    keys_padded = jnp.concatenate([zero_rim, attn_keys], axis=0)
    values_padded = jnp.concatenate([zero_rim, attn_values], axis=0)

    def one_block(number):
        offset = (number * SEG).astype(jnp.int32)
        query_rows = lax.dynamic_slice_in_dim(queries, offset, SEG, 0)
        keys_all = lax.dynamic_slice_in_dim(keys_padded, offset, SEG + WINDOW, 0)
        values_all = lax.dynamic_slice_in_dim(values_padded, offset, SEG + WINDOW, 0)
        starts = lax.dynamic_slice_in_dim(doc_start, offset, SEG, 0)
        query_pos = offset + jnp.arange(SEG, dtype=jnp.int32)
        key_pos = offset - WINDOW + jnp.arange(SEG + WINDOW, dtype=jnp.int32)
        return attend(query_rows, keys_all, values_all, sink_logits, starts, query_pos, key_pos)
    heads_out = lax.map(one_block, jnp.arange(N_SEQ, dtype=jnp.int32)).reshape(PACK, HEADS * HEAD_DIM)
    mixed = residual.astype(jnp.float32) + jnp.dot(heads_out, out_proj, preferred_element_type=jnp.float32)
    normed = (mixed * lax.rsqrt(lax.optimization_barrier(jnp.mean(mixed * mixed, axis=-1, keepdims=True)) + EPSILON) * norm_gain).astype(jnp.bfloat16)
    route_gates = route_scores / lax.optimization_barrier(jnp.sum(route_scores, axis=-1, keepdims=True))
    rows_max = N_SEQ * CAP
    block_width = FF // HID_BLOCKS

    def select(expert):
        member = expert_ids == expert
        weight_row = lax.optimization_barrier(jnp.sum(jnp.where(member, route_gates, 0.0), axis=1))
        routed = jnp.any(member, axis=1)
        count = jnp.sum(routed.astype(jnp.int32))
        picks = jnp.nonzero(routed, size=rows_max, fill_value=0)[0].astype(jnp.int32)
        live = jnp.arange(rows_max, dtype=jnp.int32) < count
        weight_live = jnp.where(live, weight_row[picks], 0.0)
        return (picks, weight_live)

    def expert_front(expert, picks):
        rows = normed[picks]
        gate_value = jnp.dot(rows, w_gate_up[expert, 0], preferred_element_type=jnp.float32)
        up_value = jnp.dot(rows, w_gate_up[expert, 1], preferred_element_type=jnp.float32)
        return (rows, gate_value, up_value)

    def forward(moe_out, expert):
        picks, weight_live = select(expert)
        rows, gate_value, up_value = expert_front(expert, picks)
        squashed = jax.nn.sigmoid(GLU_ALPHA * gate_value)
        hidden = ((up_value + 1.0) * gate_value * squashed).astype(jnp.bfloat16)
        blocks = hidden.reshape(rows_max, HID_BLOCKS, block_width).astype(jnp.float32)
        down_blocks = w_down[expert].reshape(HID_BLOCKS, block_width, D).astype(jnp.float32)
        block_out = jnp.einsum('rbf,bfd->brd', blocks, down_blocks).astype(jnp.bfloat16)
        block_out = lax.optimization_barrier(block_out)
        summed = lax.optimization_barrier(jnp.sum(block_out.astype(jnp.float32), axis=0))
        return (moe_out.at[picks].add(weight_live[:, None] * summed), None)
    moe_out, _ = lax.scan(forward, jnp.zeros((PACK, D), jnp.float32), jnp.arange(EXPERTS, dtype=jnp.int32))
    target = STEER * control / jnp.sqrt(jnp.sum(control * control))
    residual_error = mixed + moe_out - target[None, :]

    def backward(carry, expert):
        picks, weight_live = select(expert)
        rows, gate_value, up_value = expert_front(expert, picks)
        squashed = jax.nn.sigmoid(GLU_ALPHA * gate_value)
        d_out = (weight_live[:, None] * residual_error[picks]).astype(jnp.bfloat16)
        d_hidden = jnp.dot(d_out, w_down[expert].T, preferred_element_type=jnp.float32)
        d_gate = (d_hidden * (up_value + 1.0) * (squashed + GLU_ALPHA * gate_value * squashed * (1.0 - squashed))).astype(jnp.bfloat16)
        d_up = (d_hidden * gate_value * squashed).astype(jnp.bfloat16)
        grad_gate = jnp.dot(rows.T, d_gate, preferred_element_type=jnp.float32)
        grad_up = jnp.dot(rows.T, d_up, preferred_element_type=jnp.float32)
        return (carry, jnp.stack([grad_gate, grad_up]).astype(jnp.bfloat16))
    _, grads = lax.scan(backward, jnp.zeros((), jnp.float32), jnp.arange(EXPERTS, dtype=jnp.int32))
    return grads
```

```python
import functools

import jax
import jax.numpy as jnp
from jax import lax
from jax.experimental import pallas as pl
from jax.experimental.pallas import tpu as pltpu
from jax.sharding import PartitionSpec as P

D = 2880
HEAD_DIM = 64
WINDOW = 128
TOPK = 4


GLU_ALPHA = 1.702
STEER = 6.5
EPSILON = 1e-05
MASKED = -1e30
MESH = pl.DeviceIdType.MESH


def passed_along(block, axis, distance):
    devices = range(lax.axis_size(axis))
    route = [(i - distance, i) for i in devices if i - distance in devices]
    return lax.ppermute(block, axis, route)


def attend(queries, attn_keys, attn_values, sink_logits, doc_start):
    seg_len = queries.shape[0]
    heads_here = queries.shape[1] // HEAD_DIM
    kv_here = attn_keys.shape[1] // HEAD_DIM
    group_size = heads_here // kv_here
    both_rims = passed_along(jnp.stack([attn_keys, attn_values]), "seq", 1)
    keys_all = jnp.concatenate([both_rims[0], attn_keys], axis=0).reshape(
        WINDOW + seg_len, kv_here, HEAD_DIM
    )
    values_all = jnp.concatenate([both_rims[1], attn_values], axis=0).reshape(
        WINDOW + seg_len, kv_here, HEAD_DIM
    )
    offset = lax.axis_index("seq") * seg_len
    query_pos = offset + jnp.arange(seg_len, dtype=jnp.int32)
    key_pos = offset - WINDOW + jnp.arange(WINDOW + seg_len, dtype=jnp.int32)
    allowed = (
        (key_pos[None, :] <= query_pos[:, None])
        & (key_pos[None, :] > query_pos[:, None] - WINDOW)
        & (key_pos[None, :] >= doc_start[:, None])
    )
    grouped = queries.reshape(seg_len, kv_here, group_size, HEAD_DIM)
    scores = jnp.einsum(
        "qcgd,kcd->cgqk", grouped, keys_all, preferred_element_type=jnp.float32
    ) * HEAD_DIM ** (-0.5)
    masked_scores = jnp.where(allowed[None, None], scores, MASKED)
    sink_grid = sink_logits.reshape(kv_here, group_size, 1, 1)
    row_top = jnp.maximum(jnp.max(masked_scores, axis=-1, keepdims=True), sink_grid)
    expo_scores = jnp.where(allowed[None, None], jnp.exp(masked_scores - row_top), 0.0)
    denominator = jnp.sum(expo_scores, axis=-1, keepdims=True) + jnp.exp(sink_grid - row_top)
    attn_weights = (expo_scores / denominator).astype(jnp.bfloat16)
    mixed_heads = jnp.einsum(
        "cgqk,kcd->qcgd", attn_weights, values_all, preferred_element_type=jnp.float32
    )
    return mixed_heads.astype(jnp.bfloat16).reshape(seg_len, heads_here * HEAD_DIM)


def slice_total(partial_value):
    return lax.psum(partial_value, "exp")


def to_owners(buffer):
    return lax.all_to_all(buffer, "seq", split_axis=0, concat_axis=0, tiled=True)


def gather_outputs(out_part, flat_ids, slot_rank, capacity):
    width = out_part.shape[-1]
    returned = lax.all_to_all(out_part, "seq", split_axis=0, concat_axis=0, tiled=True).reshape(
        -1, width
    )
    return returned[flat_ids * capacity + slot_rank].astype(jnp.float32)


def flipped(index, bit):
    return index + bit - 2 * bit * ((index // bit) % 2)


class Links:
    def __init__(self, send_sem, recv_sem):
        self.send_sem, self.recv_sem = send_sem, recv_sem
        self.me = lax.axis_index("seq")
        self.e = lax.axis_index("exp")
        self.partner = flipped(self.me, 1)
        self.across_x = flipped(self.me, 2)
        self.across_y = flipped(self.me, 4)
        self.diagonal = flipped(self.across_x, 4)
        self.count = 0
        self.started = []

    def new(self, number=1):
        first = self.count
        self.count += number
        return first

    def copy(self, src, dst, index, seq=None, exp=None):
        device = {"seq": self.me if seq is None else seq, "exp": self.e if exp is None else exp}
        return pltpu.make_async_remote_copy(
            src_ref=src,
            dst_ref=dst,
            send_sem=self.send_sem.at[index],
            recv_sem=self.recv_sem.at[index],
            device_id=device,
            device_id_type=MESH,
        )

    def send(self, src, dst, index, **to):
        sent = self.copy(src, dst, index, **to)
        sent.start()
        self.started.append(sent)

    def arrived(self, dst, index):
        self.copy(dst, dst, index, seq=self.partner).wait_recv()

    def drain(self):
        for sent in self.started:
            sent.wait_send()


def piece_of(e, k):
    out = e
    bit = 1
    while bit <= k:
        if k & bit:
            out = flipped(out, bit)
        bit *= 2
    return out


def greet(links, n_exp, all_seq, n_seq):
    barrier = pltpu.get_barrier_semaphore()
    peers = 0
    flips = range(1, n_seq) if all_seq else [1, 2, 4]
    for k in flips:
        pl.semaphore_signal(
            barrier, inc=1, device_id={"seq": piece_of(links.me, k), "exp": links.e}, device_id_type=MESH
        )
        peers += 1
    for k in range(1, n_exp):
        pl.semaphore_signal(
            barrier, inc=1, device_id={"seq": links.me, "exp": piece_of(links.e, k)}, device_id_type=MESH
        )
        peers += 1
    pl.semaphore_wait(barrier, peers)


def spread(links, n_exp, own, everywhere, local_sem):
    me, e = links.me, links.e
    X, Y, C, D = links.across_x, links.across_y, links.partner, links.diagonal
    z_id, x_id, y_id, c_id = (links.new(n_exp) for _ in range(4))
    d_id, cx_id, cy_id, cd_id = (links.new(n_exp) for _ in range(4))
    local = pltpu.make_async_copy(own, everywhere.at[me, e], local_sem)
    local.start()

    def launch(k):
        spot = everywhere.at[me, piece_of(e, k)]
        if k:
            links.arrived(spot, z_id + k)
        src = spot if k else own
        links.send(src, spot, x_id + k, seq=X)
        links.send(src, spot, y_id + k, seq=Y)
        links.send(src, spot, c_id + k, seq=C)

    def relay(k):
        from_x = everywhere.at[X, piece_of(e, k)]
        from_y = everywhere.at[Y, piece_of(e, k)]
        links.arrived(from_x, x_id + k)
        if k % 2 == 0:
            links.send(from_x, from_x, d_id + k, seq=Y)
        links.send(from_x, from_x, cx_id + k, seq=C)
        links.arrived(from_y, y_id + k)
        if k % 2:
            links.send(from_y, from_y, d_id + k, seq=X)
        links.send(from_y, from_y, cy_id + k, seq=C)

    def last(k):
        from_d = everywhere.at[D, piece_of(e, k)]
        links.arrived(from_d, d_id + k)
        links.send(from_d, from_d, cd_id + k, seq=C)

    launch(0)
    for k in range(1, n_exp):
        links.send(own, everywhere.at[me, e], z_id + k, exp=piece_of(e, k))
    for k in range(1, n_exp):
        launch(k)
        relay(k - 1)
        if k > 1:
            last(k - 2)
    relay(n_exp - 1)
    for k in range(max(n_exp - 2, 0), n_exp):
        last(k)
    for k in range(n_exp):
        piece = piece_of(e, k)
        links.arrived(everywhere.at[C, piece], c_id + k)
        links.arrived(everywhere.at[flipped(C, 2), piece], cx_id + k)
        links.arrived(everywhere.at[flipped(C, 4), piece], cy_id + k)
        links.arrived(everywhere.at[flipped(flipped(C, 2), 4), piece], cd_id + k)
    local.wait()


def mix_kernel(
    n_seq, n_exp, part, gates, gain, everywhere, mixed_out, gates_out, landed, own, send_sem, recv_sem, local_sem
):
    links = Links(send_sem, recv_sem)
    me, e = links.me, links.e
    greet(links, n_exp, True, n_seq)
    r_id, g_id = links.new(n_exp), links.new(n_seq)
    for k in range(1, n_exp):
        links.send(part.at[piece_of(e, k)], landed.at[k - 1], r_id + k, exp=piece_of(e, k))
    for k in range(1, n_seq):
        peer = piece_of(me, k)
        links.send(gates.at[peer], gates_out.at[me], g_id + k, seq=peer)
    gates_out[me] = gates[me]
    total = part[e].astype(jnp.float32)
    for k in range(1, n_exp):
        links.arrived(landed.at[k - 1], r_id + k)
        total = total + landed[k - 1].astype(jnp.float32)
    mixed_out[...] = total
    scale = lax.rsqrt(jnp.mean(total * total, axis=-1, keepdims=True) + EPSILON)
    own[...] = (total * scale * gain[...]).astype(jnp.bfloat16)
    spread(links, n_exp, own, everywhere, local_sem)
    for k in range(1, n_seq):
        links.arrived(gates_out.at[piece_of(me, k)], g_id + k)
    links.drain()


def error_kernel(
    n_exp, part, mixed, target, everywhere, pair, side, from_x, from_y, landed, own, send_sem, recv_sem, local_sem
):
    links = Links(send_sem, recv_sem)
    me, e = links.me, links.e
    core, chip = me % 2, me // 2
    chip_x, chip_y = flipped(chip, 1), flipped(chip, 2)
    chip_d = flipped(chip_x, 2)
    X, Y, C = links.across_x, links.across_y, links.partner
    greet(links, n_exp, False, 0)
    p_id, d_id, x_id, y_id, z_id = (links.new(n_exp) for _ in range(5))
    order = list(range(n_exp))[::-1]
    for k in order:
        links.send(part.at[:, 1 - core, piece_of(e, k)], pair.at[k], p_id + k, seq=C)
    for k in order:
        links.arrived(pair.at[k], p_id + k)
        pair[k] = (pair[k].astype(jnp.float32) + part[:, core, piece_of(e, k)].astype(jnp.float32)).astype(
            jnp.bfloat16
        )
        if k % 2 == 0:
            links.send(pair.at[k, chip_d], side.at[k], d_id + k, seq=X)
            links.send(pair.at[k, chip_x], from_x.at[k], x_id + k, seq=X)
        else:
            links.send(pair.at[k, chip_d], side.at[k], d_id + k, seq=Y)
            links.send(pair.at[k, chip_y], from_y.at[k], y_id + k, seq=Y)
    for k in order:
        links.arrived(side.at[k], d_id + k)
        onward = chip_y if k % 2 == 0 else chip_x
        side[k] = (side[k].astype(jnp.float32) + pair[k, onward].astype(jnp.float32)).astype(jnp.bfloat16)
        if k % 2 == 0:
            links.send(side.at[k], from_y.at[k], y_id + k, seq=Y)
        else:
            links.send(side.at[k], from_x.at[k], x_id + k, seq=X)
    total = None
    for k in order:
        links.arrived(from_x.at[k], x_id + k)
        links.arrived(from_y.at[k], y_id + k)
        total = (
            pair[k, chip].astype(jnp.float32)
            + from_x[k].astype(jnp.float32)
            + from_y[k].astype(jnp.float32)
        )
        if k:
            from_x[k] = total.astype(jnp.bfloat16)
            links.send(from_x.at[k], landed.at[k - 1], z_id + k, exp=piece_of(e, k))
    total = total + mixed[...] - target[...]
    for k in order[:-1]:
        links.arrived(landed.at[k - 1], z_id + k)
        total = total + landed[k - 1].astype(jnp.float32)
    own[...] = total.astype(jnp.bfloat16)
    spread(links, n_exp, own, everywhere, local_sem)
    links.drain()


VM = pl.BlockSpec(memory_space=pltpu.VMEM)
ANY = pl.BlockSpec(memory_space=pl.ANY)


def dense(
    heads_out, out_proj, residual, norm_gain, expert_ids, route_scores, w_gate_up, w_down, control
):
    n_seq, n_exp = lax.axis_size("seq"), lax.axis_size("exp")
    seg_len, width = heads_out.shape[0], out_proj.shape[1]
    sub = seg_len // n_exp
    bf16, f32 = jnp.bfloat16, jnp.float32
    partial_value = jnp.dot(heads_out, out_proj, preferred_element_type=f32)
    column_width = residual.shape[1]
    at = lax.axis_index("exp") * column_width
    placed = lax.dynamic_update_slice_in_dim(jnp.zeros((seg_len, width), bf16), residual, at, 1)
    part = (partial_value + placed.astype(f32)).astype(bf16).reshape(n_exp, sub, width)
    route_gates = route_scores / jnp.sum(route_scores, axis=-1, keepdims=True)
    member = expert_ids[None, :, :] == jnp.arange(n_seq, dtype=jnp.int32)[:, None, None]
    gates = jnp.sum(jnp.where(member, route_gates[None], 0.0), axis=-1).reshape(n_seq, 1, seg_len)
    spread_count = 8 * n_exp
    rows, mixed, gates_mine = pl.pallas_call(
        functools.partial(mix_kernel, n_seq, n_exp),
        out_shape=(
            jax.ShapeDtypeStruct((n_seq, n_exp, sub, width), bf16),
            jax.ShapeDtypeStruct((sub, width), f32),
            jax.ShapeDtypeStruct((n_seq, 1, seg_len), f32),
        ),
        in_specs=[VM, VM, VM],
        out_specs=(ANY, VM, VM),
        scratch_shapes=[
            pltpu.VMEM((n_exp - 1, sub, width), bf16),
            pltpu.VMEM((sub, width), bf16),
            pltpu.SemaphoreType.DMA((spread_count + n_exp + n_seq,)),
            pltpu.SemaphoreType.DMA((spread_count + n_exp + n_seq,)),
            pltpu.SemaphoreType.DMA,
        ],
        compiler_params=pltpu.CompilerParams(collective_id=0, has_side_effects=True),
        name="mix",
    )(part, gates, norm_gain.reshape(1, width))
    rows_flat = rows.reshape(n_seq * seg_len, width)
    gate_col = gates_mine.reshape(n_seq * seg_len, 1)
    down_slice = w_down[0]
    gate_value = jnp.dot(rows_flat, w_gate_up[0, 0], preferred_element_type=f32)
    up_value = jnp.dot(rows_flat, w_gate_up[0, 1], preferred_element_type=f32)
    squashed = jax.nn.sigmoid(GLU_ALPHA * gate_value)
    glu_value = gate_value * squashed
    hidden = ((up_value + 1.0) * glu_value).astype(bf16)
    out_part = (gate_col * jnp.dot(hidden, down_slice, preferred_element_type=f32)).astype(bf16)
    target = (STEER * control / jnp.sqrt(jnp.sum(control * control))).reshape(1, width)
    errors = pl.pallas_call(
        functools.partial(error_kernel, n_exp),
        out_shape=jax.ShapeDtypeStruct((n_seq, n_exp, sub, width), bf16),
        in_specs=[VM, VM, VM],
        out_specs=ANY,
        scratch_shapes=[
            pltpu.VMEM((n_exp, n_seq // 2, sub, width), bf16),
            pltpu.VMEM((n_exp, sub, width), bf16),
            pltpu.VMEM((n_exp, sub, width), bf16),
            pltpu.VMEM((n_exp, sub, width), bf16),
            pltpu.VMEM((n_exp - 1, sub, width), bf16),
            pltpu.VMEM((sub, width), bf16),
            pltpu.SemaphoreType.DMA((spread_count + 5 * n_exp,)),
            pltpu.SemaphoreType.DMA((spread_count + 5 * n_exp,)),
            pltpu.SemaphoreType.DMA,
        ],
        compiler_params=pltpu.CompilerParams(collective_id=1, has_side_effects=True),
        name="error",
    )(out_part.reshape(n_seq // 2, 2, n_exp, sub, width), mixed, target)
    grads_in = errors.reshape(n_seq * seg_len, width)
    d_hidden = gate_col * lax.dot_general(
        grads_in, down_slice, (((1,), (1,)), ((), ())), preferred_element_type=f32
    )
    d_gate = (
        d_hidden
        * (up_value + 1.0)
        * (squashed + GLU_ALPHA * gate_value * squashed * (1.0 - squashed))
    ).astype(bf16)
    d_up = (d_hidden * glu_value).astype(bf16)
    grad_gate = lax.dot_general(rows_flat, d_gate, (((0,), (0,)), ((), ())), preferred_element_type=f32)
    grad_up = lax.dot_general(rows_flat, d_up, (((0,), (0,)), ((), ())), preferred_element_type=f32)
    return jnp.stack([grad_gate, grad_up])[None].astype(bf16)


def shards(
    queries,
    attn_keys,
    attn_values,
    sink_logits,
    out_proj,
    residual,
    norm_gain,
    doc_start,
    expert_ids,
    route_scores,
    w_gate_up,
    w_down,
    control,
):
    n_seq = lax.axis_size("seq")
    seg_len = queries.shape[0]
    capacity = 2 * TOPK * seg_len // n_seq
    block_index = lax.axis_index("exp")
    heads_out = attend(queries, attn_keys, attn_values, sink_logits, doc_start)
    if n_seq == 8 and capacity >= seg_len and lax.axis_size("exp") == 4:
        return dense(
            heads_out, out_proj, residual, norm_gain, expert_ids, route_scores, w_gate_up, w_down, control
        )
    partial_value = jnp.dot(heads_out, out_proj, preferred_element_type=jnp.float32)
    column_width = residual.shape[1]
    own_columns = lax.dynamic_slice_in_dim(
        partial_value, block_index * column_width, column_width, 1
    ) + residual.astype(jnp.float32)
    partial_value = lax.dynamic_update_slice_in_dim(
        partial_value, own_columns, block_index * column_width, 1
    )
    mixed = slice_total(partial_value)
    normed = (
        mixed * lax.rsqrt(jnp.mean(mixed * mixed, axis=-1, keepdims=True) + EPSILON) * norm_gain
    ).astype(jnp.bfloat16)
    route_gates = route_scores / jnp.sum(route_scores, axis=-1, keepdims=True)
    flat_ids = expert_ids.reshape(-1)
    onehot = (flat_ids[:, None] == jnp.arange(n_seq, dtype=jnp.int32)[None, :]).astype(jnp.int32)
    slot_rank = jnp.sum((jnp.cumsum(onehot, axis=0) - 1) * onehot, axis=1)
    slot_index = flat_ids * capacity + slot_rank
    owner_row = (
        jnp.zeros((n_seq * capacity,), jnp.int32)
        .at[slot_index]
        .set(jnp.arange(seg_len * TOPK, dtype=jnp.int32))
    )
    filled = (
        jnp.zeros((n_seq * capacity,), jnp.bfloat16)
        .at[slot_index]
        .set(jnp.ones((seg_len * TOPK,), jnp.bfloat16))
    )
    sent_rows = (normed[owner_row // TOPK] * filled[:, None]).reshape(n_seq, capacity, D)
    rows_flat = to_owners(sent_rows).reshape(-1, D)
    gate_slice = w_gate_up[0, 0]
    up_slice = w_gate_up[0, 1]
    down_slice = w_down[0]
    gate_value = jnp.dot(rows_flat, gate_slice, preferred_element_type=jnp.float32)
    up_value = jnp.dot(rows_flat, up_slice, preferred_element_type=jnp.float32)
    squashed = jax.nn.sigmoid(GLU_ALPHA * gate_value)
    glu_value = gate_value * squashed
    hidden = ((up_value + 1.0) * glu_value).astype(jnp.bfloat16)
    out_part = (
        jnp.dot(hidden, down_slice, preferred_element_type=jnp.float32)
        .astype(jnp.bfloat16)
        .reshape(n_seq, capacity, D)
    )
    picked = gather_outputs(out_part, flat_ids, slot_rank, capacity).reshape(seg_len, TOPK, D)
    moe_out = slice_total(jnp.sum(route_gates[:, :, None] * picked, axis=1))
    target = STEER * control / jnp.sqrt(jnp.sum(control * control))
    residual_error = mixed + moe_out - target[None, :]
    d_out = (
        (route_gates[:, :, None] * residual_error[:, None, :])
        .astype(jnp.bfloat16)
        .reshape(seg_len * TOPK, D)
    )
    sent_back = (d_out[owner_row] * filled[:, None]).reshape(n_seq, capacity, D)
    grads_in = to_owners(sent_back).reshape(-1, D)
    d_hidden = lax.dot_general(
        grads_in, down_slice, (((1,), (1,)), ((), ())), preferred_element_type=jnp.float32
    )
    d_gate = (
        d_hidden
        * (up_value + 1.0)
        * (squashed + GLU_ALPHA * gate_value * squashed * (1.0 - squashed))
    ).astype(jnp.bfloat16)
    d_up = (d_hidden * glu_value).astype(jnp.bfloat16)
    grad_gate = lax.dot_general(
        rows_flat, d_gate, (((0,), (0,)), ((), ())), preferred_element_type=jnp.float32
    )
    grad_up = lax.dot_general(
        rows_flat, d_up, (((0,), (0,)), ((), ())), preferred_element_type=jnp.float32
    )
    return jnp.stack([grad_gate, grad_up])[None].astype(jnp.bfloat16)


def solution(mesh):
    return jax.shard_map(
        shards,
        mesh=mesh,
        in_specs=(
            P("seq", "exp"),
            P("seq", "exp"),
            P("seq", "exp"),
            P("exp"),
            P("exp", None),
            P("seq", "exp"),
            P(),
            P("seq"),
            P("seq", None),
            P("seq", None),
            P("seq", None, None, "exp"),
            P("seq", "exp", None),
            P(),
        ),
        out_specs=P("seq", None, None, "exp"),
        check_vma=False,
    )
```

```python
import functools

import jax
import jax.numpy as jnp
from jax import lax
from jax.experimental import pallas as pl
from jax.experimental.pallas import tpu as pltpu
from jax.sharding import PartitionSpec as P

D = 2880
HEAD_DIM = 64
WINDOW = 128
TOPK = 4


GLU_ALPHA = 1.702
STEER = 6.5
EPSILON = 1e-05
MASKED = -1e30
MESH = pl.DeviceIdType.MESH


def passed_along(block, axis, distance):
    devices = range(lax.axis_size(axis))
    route = [(i - distance, i) for i in devices if i - distance in devices]
    return lax.ppermute(block, axis, route)


def attend(queries, attn_keys, attn_values, sink_logits, doc_start):
    seg_len = queries.shape[0]
    heads_here = queries.shape[1] // HEAD_DIM
    kv_here = attn_keys.shape[1] // HEAD_DIM
    group_size = heads_here // kv_here
    both_rims = passed_along(jnp.stack([attn_keys, attn_values]), "seq", 1)
    keys_all = jnp.concatenate([both_rims[0], attn_keys], axis=0).reshape(
        WINDOW + seg_len, kv_here, HEAD_DIM
    )
    values_all = jnp.concatenate([both_rims[1], attn_values], axis=0).reshape(
        WINDOW + seg_len, kv_here, HEAD_DIM
    )
    offset = lax.axis_index("seq") * seg_len
    query_pos = offset + jnp.arange(seg_len, dtype=jnp.int32)
    key_pos = offset - WINDOW + jnp.arange(WINDOW + seg_len, dtype=jnp.int32)
    allowed = (
        (key_pos[None, :] <= query_pos[:, None])
        & (key_pos[None, :] > query_pos[:, None] - WINDOW)
        & (key_pos[None, :] >= doc_start[:, None])
    )
    grouped = queries.reshape(seg_len, kv_here, group_size, HEAD_DIM)
    scores = jnp.einsum(
        "qcgd,kcd->cgqk", grouped, keys_all, preferred_element_type=jnp.float32
    ) * HEAD_DIM ** (-0.5)
    masked_scores = jnp.where(allowed[None, None], scores, MASKED)
    sink_grid = sink_logits.reshape(kv_here, group_size, 1, 1)
    row_top = jnp.maximum(jnp.max(masked_scores, axis=-1, keepdims=True), sink_grid)
    expo_scores = jnp.where(allowed[None, None], jnp.exp(masked_scores - row_top), 0.0)
    denominator = jnp.sum(expo_scores, axis=-1, keepdims=True) + jnp.exp(sink_grid - row_top)
    attn_weights = (expo_scores / denominator).astype(jnp.bfloat16)
    mixed_heads = jnp.einsum(
        "cgqk,kcd->qcgd", attn_weights, values_all, preferred_element_type=jnp.float32
    )
    return mixed_heads.astype(jnp.bfloat16).reshape(seg_len, heads_here * HEAD_DIM)


def slice_total(partial_value):
    return lax.psum(partial_value, "exp")


def to_owners(buffer):
    return lax.all_to_all(buffer, "seq", split_axis=0, concat_axis=0, tiled=True)


def gather_outputs(out_part, flat_ids, slot_rank, capacity):
    width = out_part.shape[-1]
    returned = lax.all_to_all(out_part, "seq", split_axis=0, concat_axis=0, tiled=True).reshape(
        -1, width
    )
    return returned[flat_ids * capacity + slot_rank].astype(jnp.float32)


def flipped(index, bit):
    return index + bit - 2 * bit * ((index // bit) % 2)


class Links:
    def __init__(self, send_sem, recv_sem):
        self.send_sem, self.recv_sem = send_sem, recv_sem
        self.me = lax.axis_index("seq")
        self.e = lax.axis_index("exp")
        self.partner = flipped(self.me, 1)
        self.across_x = flipped(self.me, 2)
        self.across_y = flipped(self.me, 4)
        self.diagonal = flipped(self.across_x, 4)
        self.count = 0
        self.started = []

    def new(self, number=1):
        first = self.count
        self.count += number
        return first

    def copy(self, src, dst, index, seq=None, exp=None):
        device = {"seq": self.me if seq is None else seq, "exp": self.e if exp is None else exp}
        return pltpu.make_async_remote_copy(
            src_ref=src,
            dst_ref=dst,
            send_sem=self.send_sem.at[index],
            recv_sem=self.recv_sem.at[index],
            device_id=device,
            device_id_type=MESH,
        )

    def send(self, src, dst, index, **to):
        sent = self.copy(src, dst, index, **to)
        sent.start()
        self.started.append(sent)

    def arrived(self, dst, index):
        self.copy(dst, dst, index, seq=self.partner).wait_recv()

    def drain(self):
        for sent in self.started:
            sent.wait_send()


def piece_of(e, k):
    out = e
    bit = 1
    while bit <= k:
        if k & bit:
            out = flipped(out, bit)
        bit *= 2
    return out


def greet(links, n_exp, all_seq, n_seq):
    barrier = pltpu.get_barrier_semaphore()
    peers = 0
    flips = range(1, n_seq) if all_seq else [1, 2, 4]
    for k in flips:
        pl.semaphore_signal(
            barrier, inc=1, device_id={"seq": piece_of(links.me, k), "exp": links.e}, device_id_type=MESH
        )
        peers += 1
    for k in range(1, n_exp):
        pl.semaphore_signal(
            barrier, inc=1, device_id={"seq": links.me, "exp": piece_of(links.e, k)}, device_id_type=MESH
        )
        peers += 1
    pl.semaphore_wait(barrier, peers)


def spread(links, n_exp, own, everywhere, local_sem, consume):
    me, e = links.me, links.e
    X, Y, C, D = links.across_x, links.across_y, links.partner, links.diagonal
    z_id, x_id, y_id, c_id = (links.new(n_exp) for _ in range(4))
    d_id, cx_id, cy_id, cd_id = (links.new(n_exp) for _ in range(4))
    local = pltpu.make_async_copy(own, everywhere.at[e, me], local_sem)
    local.start()

    def launch(k):
        spot = everywhere.at[piece_of(e, k), me]
        if k:
            links.arrived(spot, z_id + k)
        src = spot if k else own
        links.send(src, spot, x_id + k, seq=X)
        links.send(src, spot, y_id + k, seq=Y)
        links.send(src, spot, c_id + k, seq=C)

    def relay(k):
        from_x = everywhere.at[piece_of(e, k), X]
        from_y = everywhere.at[piece_of(e, k), Y]
        links.arrived(from_x, x_id + k)
        if k % 2 == 0:
            links.send(from_x, from_x, d_id + k, seq=Y)
        links.send(from_x, from_x, cx_id + k, seq=C)
        links.arrived(from_y, y_id + k)
        if k % 2:
            links.send(from_y, from_y, d_id + k, seq=X)
        links.send(from_y, from_y, cy_id + k, seq=C)

    def last(k):
        from_d = everywhere.at[piece_of(e, k), D]
        links.arrived(from_d, d_id + k)
        links.send(from_d, from_d, cd_id + k, seq=C)

    def finish(k):
        piece = everywhere.at[piece_of(e, k)]
        links.arrived(piece.at[C], c_id + k)
        links.arrived(piece.at[flipped(C, 2)], cx_id + k)
        links.arrived(piece.at[flipped(C, 4)], cy_id + k)
        links.arrived(piece.at[flipped(flipped(C, 2), 4)], cd_id + k)
        if k == 0:
            local.wait()
        consume(k)

    launch(0)
    for k in range(1, n_exp):
        links.send(own, everywhere.at[e, me], z_id + k, exp=piece_of(e, k))
    for k in range(1, n_exp):
        launch(k)
        relay(k - 1)
        if k > 1:
            last(k - 2)
    relay(n_exp - 1)
    last(n_exp - 2)
    finish(0)
    last(n_exp - 1)
    for k in range(1, n_exp):
        finish(k)


def tile_of(size, most=256):
    return next(t for t in range(most, 0, -1) if size % t == 0 and t % 16 == 0)


def times_rows(weights, rows):
    return lax.dot_general(weights, rows, (((1,), (1,)), ((), ())), preferred_element_type=jnp.float32)


def mix_kernel(
    n_seq,
    n_exp,
    part,
    gates,
    gain,
    weights_in,
    rows_out,
    mixed_out,
    gates_out,
    hidden_out,
    by_gate_out,
    by_up_out,
    weights,
    everywhere,
    landed,
    own,
    send_sem,
    recv_sem,
    local_sem,
    rows_sem,
):
    links = Links(send_sem, recv_sem)
    me, e = links.me, links.e
    load = pltpu.make_async_copy(weights_in, weights, local_sem.at[1])
    load.start()
    greet(links, n_exp, True, n_seq)
    r_id, g_id = links.new(n_exp), links.new(n_seq)
    for k in range(1, n_exp):
        links.send(part.at[piece_of(e, k)], landed.at[k - 1], r_id + k, exp=piece_of(e, k))
    for k in range(1, n_seq):
        peer = piece_of(me, k)
        links.send(gates.at[peer], gates_out.at[me], g_id + k, seq=peer)
    gates_out[me] = gates[me]
    total = part[e].astype(jnp.float32)
    for k in range(1, n_exp):
        links.arrived(landed.at[k - 1], r_id + k)
        total = total + landed[k - 1].astype(jnp.float32)
    mixed_out[...] = total
    scale = lax.rsqrt(jnp.mean(total * total, axis=-1, keepdims=True) + EPSILON)
    own[...] = (total * scale * gain[...]).astype(jnp.bfloat16)
    ff, width = weights.shape[1:]
    tile = tile_of(ff)
    stores = []

    def consume(k):
        piece = piece_of(e, k)
        if k == 0:
            load.wait()
        store = pltpu.make_async_copy(everywhere.at[piece], rows_out.at[piece], rows_sem.at[k])
        store.start()
        stores.append(store)

        def step(index, carry):
            at = pl.ds(pl.multiple_of(index * tile, 16), tile)
            rows = everywhere[piece].reshape(-1, width)
            gate_value = times_rows(weights[0, at, :], rows)
            up_value = times_rows(weights[1, at, :], rows)
            squashed = jax.nn.sigmoid(GLU_ALPHA * gate_value)
            glu_value = gate_value * squashed
            hidden_out[piece, at, :] = ((up_value + 1.0) * glu_value).astype(jnp.bfloat16)
            by_gate_out[piece, at, :] = (up_value + 1.0) * (
                squashed + GLU_ALPHA * gate_value * squashed * (1.0 - squashed)
            )
            by_up_out[piece, at, :] = glu_value
            return carry

        lax.fori_loop(0, ff // tile, step, 0)

    spread(links, n_exp, own, everywhere, local_sem.at[0], consume)
    for k in range(1, n_seq):
        links.arrived(gates_out.at[piece_of(me, k)], g_id + k)
    links.drain()
    for store in stores:
        store.wait()


def error_kernel(
    n_seq,
    n_exp,
    hidden,
    gate_col,
    gate_row,
    weights,
    by_gate_in,
    by_up_in,
    mixed,
    target,
    grads_out,
    factors,
    everywhere,
    part,
    pair,
    side,
    from_x,
    from_y,
    landed,
    own,
    send_sem,
    recv_sem,
    local_sem,
):
    links = Links(send_sem, recv_sem)
    me, e = links.me, links.e
    core, chip = me % 2, me // 2
    chip_x, chip_y = flipped(chip, 1), flipped(chip, 2)
    chip_d = flipped(chip_x, 2)
    X, Y, C = links.across_x, links.across_y, links.partner
    ff, width = weights.shape
    sub = mixed.shape[0]
    tile = tile_of(ff)
    loads = [
        pltpu.make_async_copy(ref, factors.at[number], local_sem.at[1 + number])
        for number, ref in enumerate((by_gate_in, by_up_in))
    ]
    for load in loads:
        load.start()
    greet(links, n_exp, False, 0)
    p_id, d_id, x_id, y_id, z_id = (links.new(n_exp) for _ in range(5))
    order = list(range(n_exp))[::-1]

    def produce(k):
        piece = piece_of(e, k)
        for start in range(0, width, 512):
            columns = slice(start, min(width, start + 512))
            outs = lax.dot_general(
                hidden[piece], weights[:, columns], (((0,), (0,)), ((), ())), preferred_element_type=jnp.float32
            )
            outs = (outs * gate_col[piece]).astype(jnp.bfloat16)
            part[k, :, :, :, columns] = outs.reshape(n_seq // 2, 2, sub, -1)
        links.send(part.at[k, :, 1 - core], pair.at[k], p_id + k, seq=C)

    def merge(k):
        links.arrived(pair.at[k], p_id + k)
        pair[k] = (pair[k].astype(jnp.float32) + part[k, :, core].astype(jnp.float32)).astype(jnp.bfloat16)
        if k % 2 == 0:
            links.send(pair.at[k, chip_d], side.at[k], d_id + k, seq=X)
            links.send(pair.at[k, chip_x], from_x.at[k], x_id + k, seq=X)
        else:
            links.send(pair.at[k, chip_d], side.at[k], d_id + k, seq=Y)
            links.send(pair.at[k, chip_y], from_y.at[k], y_id + k, seq=Y)

    def pass_on(k):
        links.arrived(side.at[k], d_id + k)
        onward = chip_y if k % 2 == 0 else chip_x
        side[k] = (side[k].astype(jnp.float32) + pair[k, onward].astype(jnp.float32)).astype(jnp.bfloat16)
        if k % 2 == 0:
            links.send(side.at[k], from_y.at[k], y_id + k, seq=Y)
        else:
            links.send(side.at[k], from_x.at[k], x_id + k, seq=X)

    def collect(k):
        links.arrived(from_x.at[k], x_id + k)
        links.arrived(from_y.at[k], y_id + k)
        total = (
            pair[k, chip].astype(jnp.float32)
            + from_x[k].astype(jnp.float32)
            + from_y[k].astype(jnp.float32)
        )
        if k:
            from_x[k] = total.astype(jnp.bfloat16)
            links.send(from_x.at[k], landed.at[k - 1], z_id + k, exp=piece_of(e, k))
        return total

    produce(order[0])
    for before, k in zip(order, order[1:]):
        produce(k)
        merge(before)
    merge(order[-1])
    pass_on(order[0])
    for before, k in zip(order, order[1:]):
        pass_on(k)
        collect(before)
    total = collect(0) + mixed[...] - target[...]
    for k in order[:-1]:
        links.arrived(landed.at[k - 1], z_id + k)
        total = total + landed[k - 1].astype(jnp.float32)
    own[...] = total.astype(jnp.bfloat16)
    for load in loads:
        load.wait()

    def consume(k):
        piece = piece_of(e, k)
        lanes = pl.ds(pl.multiple_of(piece * (n_seq * sub), n_seq * sub), n_seq * sub)

        def step(index, carry):
            at = pl.ds(pl.multiple_of(index * tile, 16), tile)
            d_hidden = times_rows(weights[at, :], everywhere[piece].reshape(-1, width)) * gate_row[piece]
            grads_out[0, at, lanes] = (d_hidden * factors[0, piece, at, :]).astype(jnp.bfloat16)
            grads_out[1, at, lanes] = (d_hidden * factors[1, piece, at, :]).astype(jnp.bfloat16)
            return carry

        lax.fori_loop(0, ff // tile, step, 0)

    spread(links, n_exp, own, everywhere, local_sem.at[0], consume)
    links.drain()


VM = pl.BlockSpec(memory_space=pltpu.VMEM)
ANY = pl.BlockSpec(memory_space=pl.ANY)


def dense(
    heads_out, out_proj, residual, norm_gain, expert_ids, route_scores, w_gate_up, w_down, control
):
    n_seq, n_exp = lax.axis_size("seq"), lax.axis_size("exp")
    seg_len, width = heads_out.shape[0], out_proj.shape[1]
    sub = seg_len // n_exp
    bf16, f32 = jnp.bfloat16, jnp.float32
    partial_value = jnp.dot(heads_out, out_proj, preferred_element_type=f32)
    column_width = residual.shape[1]
    at = lax.axis_index("exp") * column_width
    placed = lax.dynamic_update_slice_in_dim(jnp.zeros((seg_len, width), bf16), residual, at, 1)
    part = (partial_value + placed.astype(f32)).astype(bf16).reshape(n_exp, sub, width)
    route_gates = route_scores / jnp.sum(route_scores, axis=-1, keepdims=True)
    member = expert_ids[None, :, :] == jnp.arange(n_seq, dtype=jnp.int32)[:, None, None]
    gates = jnp.sum(jnp.where(member, route_gates[None], 0.0), axis=-1).reshape(n_seq, 1, seg_len)
    spread_count = 8 * n_exp
    ff = w_down.shape[1]
    group = n_seq * sub
    rows, mixed, gates_mine, hidden, by_gate, by_up = pl.pallas_call(
        functools.partial(mix_kernel, n_seq, n_exp),
        out_shape=(
            jax.ShapeDtypeStruct((n_exp, n_seq, sub, width), bf16),
            jax.ShapeDtypeStruct((sub, width), f32),
            jax.ShapeDtypeStruct((n_seq, 1, seg_len), f32),
            jax.ShapeDtypeStruct((n_exp, ff, group), bf16),
            jax.ShapeDtypeStruct((n_exp, ff, group), f32),
            jax.ShapeDtypeStruct((n_exp, ff, group), f32),
        ),
        in_specs=[VM, VM, VM, ANY],
        out_specs=(ANY, VM, VM, VM, VM, VM),
        scratch_shapes=[
            pltpu.VMEM((2, ff, width), bf16),
            pltpu.VMEM((n_exp, n_seq, sub, width), bf16),
            pltpu.VMEM((n_exp - 1, sub, width), bf16),
            pltpu.VMEM((sub, width), bf16),
            pltpu.SemaphoreType.DMA((spread_count + n_exp + n_seq,)),
            pltpu.SemaphoreType.DMA((spread_count + n_exp + n_seq,)),
            pltpu.SemaphoreType.DMA((2,)),
            pltpu.SemaphoreType.DMA((n_exp,)),
        ],
        compiler_params=pltpu.CompilerParams(collective_id=0, has_side_effects=True),
        name="mix",
    )(part, gates, norm_gain.reshape(1, width), jnp.swapaxes(w_gate_up[0], 1, 2))
    gate_flat = gates_mine.reshape(n_seq, n_exp, sub).transpose(1, 0, 2).reshape(n_exp, group)
    target = (STEER * control / jnp.sqrt(jnp.sum(control * control))).reshape(1, width)
    d_both = pl.pallas_call(
        functools.partial(error_kernel, n_seq, n_exp),
        out_shape=jax.ShapeDtypeStruct((2, ff, n_exp * group), bf16),
        in_specs=[VM, VM, VM, VM, ANY, ANY, VM, VM],
        out_specs=VM,
        scratch_shapes=[
            pltpu.VMEM((2, n_exp, ff, group), f32),
            pltpu.VMEM((n_exp, n_seq, sub, width), bf16),
            pltpu.VMEM((n_exp, n_seq // 2, 2, sub, width), bf16),
            pltpu.VMEM((n_exp, n_seq // 2, sub, width), bf16),
            pltpu.VMEM((n_exp, sub, width), bf16),
            pltpu.VMEM((n_exp, sub, width), bf16),
            pltpu.VMEM((n_exp, sub, width), bf16),
            pltpu.VMEM((n_exp - 1, sub, width), bf16),
            pltpu.VMEM((sub, width), bf16),
            pltpu.SemaphoreType.DMA((spread_count + 5 * n_exp,)),
            pltpu.SemaphoreType.DMA((spread_count + 5 * n_exp,)),
            pltpu.SemaphoreType.DMA((3,)),
        ],
        compiler_params=pltpu.CompilerParams(collective_id=1, has_side_effects=True),
        name="error",
    )(hidden, gate_flat[:, :, None], gate_flat[:, None, :], w_down[0], by_gate, by_up, mixed, target)
    grads = lax.dot_general(
        d_both.reshape(2 * ff, n_exp * group),
        rows.reshape(n_exp * group, width),
        (((1,), (0,)), ((), ())),
        preferred_element_type=f32,
    )
    return jnp.swapaxes(grads.astype(bf16).reshape(2, ff, width), 1, 2)[None]


def shards(
    queries,
    attn_keys,
    attn_values,
    sink_logits,
    out_proj,
    residual,
    norm_gain,
    doc_start,
    expert_ids,
    route_scores,
    w_gate_up,
    w_down,
    control,
):
    n_seq = lax.axis_size("seq")
    seg_len = queries.shape[0]
    capacity = 2 * TOPK * seg_len // n_seq
    block_index = lax.axis_index("exp")
    heads_out = attend(queries, attn_keys, attn_values, sink_logits, doc_start)
    if n_seq == 8 and capacity >= seg_len and lax.axis_size("exp") == 4:
        return dense(
            heads_out, out_proj, residual, norm_gain, expert_ids, route_scores, w_gate_up, w_down, control
        )
    partial_value = jnp.dot(heads_out, out_proj, preferred_element_type=jnp.float32)
    column_width = residual.shape[1]
    own_columns = lax.dynamic_slice_in_dim(
        partial_value, block_index * column_width, column_width, 1
    ) + residual.astype(jnp.float32)
    partial_value = lax.dynamic_update_slice_in_dim(
        partial_value, own_columns, block_index * column_width, 1
    )
    mixed = slice_total(partial_value)
    normed = (
        mixed * lax.rsqrt(jnp.mean(mixed * mixed, axis=-1, keepdims=True) + EPSILON) * norm_gain
    ).astype(jnp.bfloat16)
    route_gates = route_scores / jnp.sum(route_scores, axis=-1, keepdims=True)
    flat_ids = expert_ids.reshape(-1)
    onehot = (flat_ids[:, None] == jnp.arange(n_seq, dtype=jnp.int32)[None, :]).astype(jnp.int32)
    slot_rank = jnp.sum((jnp.cumsum(onehot, axis=0) - 1) * onehot, axis=1)
    slot_index = flat_ids * capacity + slot_rank
    owner_row = (
        jnp.zeros((n_seq * capacity,), jnp.int32)
        .at[slot_index]
        .set(jnp.arange(seg_len * TOPK, dtype=jnp.int32))
    )
    filled = (
        jnp.zeros((n_seq * capacity,), jnp.bfloat16)
        .at[slot_index]
        .set(jnp.ones((seg_len * TOPK,), jnp.bfloat16))
    )
    sent_rows = (normed[owner_row // TOPK] * filled[:, None]).reshape(n_seq, capacity, D)
    rows_flat = to_owners(sent_rows).reshape(-1, D)
    gate_slice = w_gate_up[0, 0]
    up_slice = w_gate_up[0, 1]
    down_slice = w_down[0]
    gate_value = jnp.dot(rows_flat, gate_slice, preferred_element_type=jnp.float32)
    up_value = jnp.dot(rows_flat, up_slice, preferred_element_type=jnp.float32)
    squashed = jax.nn.sigmoid(GLU_ALPHA * gate_value)
    glu_value = gate_value * squashed
    hidden = ((up_value + 1.0) * glu_value).astype(jnp.bfloat16)
    out_part = (
        jnp.dot(hidden, down_slice, preferred_element_type=jnp.float32)
        .astype(jnp.bfloat16)
        .reshape(n_seq, capacity, D)
    )
    picked = gather_outputs(out_part, flat_ids, slot_rank, capacity).reshape(seg_len, TOPK, D)
    moe_out = slice_total(jnp.sum(route_gates[:, :, None] * picked, axis=1))
    target = STEER * control / jnp.sqrt(jnp.sum(control * control))
    residual_error = mixed + moe_out - target[None, :]
    d_out = (
        (route_gates[:, :, None] * residual_error[:, None, :])
        .astype(jnp.bfloat16)
        .reshape(seg_len * TOPK, D)
    )
    sent_back = (d_out[owner_row] * filled[:, None]).reshape(n_seq, capacity, D)
    grads_in = to_owners(sent_back).reshape(-1, D)
    d_hidden = lax.dot_general(
        grads_in, down_slice, (((1,), (1,)), ((), ())), preferred_element_type=jnp.float32
    )
    d_gate = (
        d_hidden
        * (up_value + 1.0)
        * (squashed + GLU_ALPHA * gate_value * squashed * (1.0 - squashed))
    ).astype(jnp.bfloat16)
    d_up = (d_hidden * glu_value).astype(jnp.bfloat16)
    grad_gate = lax.dot_general(
        rows_flat, d_gate, (((0,), (0,)), ((), ())), preferred_element_type=jnp.float32
    )
    grad_up = lax.dot_general(
        rows_flat, d_up, (((0,), (0,)), ((), ())), preferred_element_type=jnp.float32
    )
    return jnp.stack([grad_gate, grad_up])[None].astype(jnp.bfloat16)


def solution(mesh):
    return jax.shard_map(
        shards,
        mesh=mesh,
        in_specs=(
            P("seq", "exp"),
            P("seq", "exp"),
            P("seq", "exp"),
            P("exp"),
            P("exp", None),
            P("seq", "exp"),
            P(),
            P("seq"),
            P("seq", None),
            P("seq", None),
            P("seq", None, None, "exp"),
            P("seq", "exp", None),
            P(),
        ),
        out_specs=P("seq", None, None, "exp"),
        check_vma=False,
    )
```

```python
import functools

import jax
import jax.numpy as jnp
from jax import lax
from jax.experimental import pallas as pl
from jax.experimental.pallas import tpu as pltpu
from jax.sharding import PartitionSpec as P

D = 2880
HEAD_DIM = 64
WINDOW = 128
TOPK = 4


GLU_ALPHA = 1.702
STEER = 6.5
EPSILON = 1e-05
MASKED = -1e30
MESH = pl.DeviceIdType.MESH


def passed_along(block, axis, distance):
    devices = range(lax.axis_size(axis))
    route = [(i - distance, i) for i in devices if i - distance in devices]
    return lax.ppermute(block, axis, route)


def attend(queries, attn_keys, attn_values, sink_logits, doc_start):
    seg_len = queries.shape[0]
    heads_here = queries.shape[1] // HEAD_DIM
    kv_here = attn_keys.shape[1] // HEAD_DIM
    group_size = heads_here // kv_here
    both_rims = passed_along(jnp.stack([attn_keys, attn_values]), "seq", 1)
    keys_all = jnp.concatenate([both_rims[0], attn_keys], axis=0).reshape(
        WINDOW + seg_len, kv_here, HEAD_DIM
    )
    values_all = jnp.concatenate([both_rims[1], attn_values], axis=0).reshape(
        WINDOW + seg_len, kv_here, HEAD_DIM
    )
    offset = lax.axis_index("seq") * seg_len
    query_pos = offset + jnp.arange(seg_len, dtype=jnp.int32)
    key_pos = offset - WINDOW + jnp.arange(WINDOW + seg_len, dtype=jnp.int32)
    allowed = (
        (key_pos[None, :] <= query_pos[:, None])
        & (key_pos[None, :] > query_pos[:, None] - WINDOW)
        & (key_pos[None, :] >= doc_start[:, None])
    )
    grouped = queries.reshape(seg_len, kv_here, group_size, HEAD_DIM)
    scores = jnp.einsum(
        "qcgd,kcd->cgqk", grouped, keys_all, preferred_element_type=jnp.float32
    ) * HEAD_DIM ** (-0.5)
    masked_scores = jnp.where(allowed[None, None], scores, MASKED)
    sink_grid = sink_logits.reshape(kv_here, group_size, 1, 1)
    row_top = jnp.maximum(jnp.max(masked_scores, axis=-1, keepdims=True), sink_grid)
    expo_scores = jnp.where(allowed[None, None], jnp.exp(masked_scores - row_top), 0.0)
    denominator = jnp.sum(expo_scores, axis=-1, keepdims=True) + jnp.exp(sink_grid - row_top)
    attn_weights = (expo_scores / denominator).astype(jnp.bfloat16)
    mixed_heads = jnp.einsum(
        "cgqk,kcd->qcgd", attn_weights, values_all, preferred_element_type=jnp.float32
    )
    return mixed_heads.astype(jnp.bfloat16).reshape(seg_len, heads_here * HEAD_DIM)


def slice_total(partial_value):
    return lax.psum(partial_value, "exp")


def to_owners(buffer):
    return lax.all_to_all(buffer, "seq", split_axis=0, concat_axis=0, tiled=True)


def gather_outputs(out_part, flat_ids, slot_rank, capacity):
    width = out_part.shape[-1]
    returned = lax.all_to_all(out_part, "seq", split_axis=0, concat_axis=0, tiled=True).reshape(
        -1, width
    )
    return returned[flat_ids * capacity + slot_rank].astype(jnp.float32)


def flipped(index, bit):
    return index + bit - 2 * bit * ((index // bit) % 2)


class Links:
    def __init__(self, send_sem, recv_sem):
        self.send_sem, self.recv_sem = send_sem, recv_sem
        self.me = lax.axis_index("seq")
        self.e = lax.axis_index("exp")
        self.partner = flipped(self.me, 1)
        self.across_x = flipped(self.me, 2)
        self.across_y = flipped(self.me, 4)
        self.diagonal = flipped(self.across_x, 4)
        self.count = 0
        self.started = []

    def new(self, number=1):
        first = self.count
        self.count += number
        return first

    def copy(self, src, dst, index, seq=None, exp=None):
        device = {"seq": self.me if seq is None else seq, "exp": self.e if exp is None else exp}
        return pltpu.make_async_remote_copy(
            src_ref=src,
            dst_ref=dst,
            send_sem=self.send_sem.at[index],
            recv_sem=self.recv_sem.at[index],
            device_id=device,
            device_id_type=MESH,
        )

    def send(self, src, dst, index, **to):
        sent = self.copy(src, dst, index, **to)
        sent.start()
        self.started.append(sent)

    def arrived(self, dst, index):
        self.copy(dst, dst, index, seq=self.partner).wait_recv()

    def drain(self):
        for sent in self.started:
            sent.wait_send()


def piece_of(e, k):
    out = e
    bit = 1
    while bit <= k:
        if k & bit:
            out = flipped(out, bit)
        bit *= 2
    return out


def greet(links, n_exp, all_seq, n_seq):
    barrier = pltpu.get_barrier_semaphore()
    peers = 0
    flips = range(1, n_seq) if all_seq else [1, 2, 4]
    for k in flips:
        pl.semaphore_signal(
            barrier, inc=1, device_id={"seq": piece_of(links.me, k), "exp": links.e}, device_id_type=MESH
        )
        peers += 1
    for k in range(1, n_exp):
        pl.semaphore_signal(
            barrier, inc=1, device_id={"seq": links.me, "exp": piece_of(links.e, k)}, device_id_type=MESH
        )
        peers += 1
    pl.semaphore_wait(barrier, peers)


def spread(links, n_exp, own, everywhere, local_sem, consume):
    me, e = links.me, links.e
    X, Y, C, D = links.across_x, links.across_y, links.partner, links.diagonal
    z_id, x_id, y_id, c_id = (links.new(n_exp) for _ in range(4))
    d_id, cx_id, cy_id, cd_id = (links.new(n_exp) for _ in range(4))
    local = pltpu.make_async_copy(own, everywhere.at[e, me], local_sem)
    local.start()

    def launch(k):
        spot = everywhere.at[piece_of(e, k), me]
        if k:
            links.arrived(spot, z_id + k)
        src = spot if k else own
        links.send(src, spot, x_id + k, seq=X)
        links.send(src, spot, y_id + k, seq=Y)
        links.send(src, spot, c_id + k, seq=C)

    def relay(k):
        from_x = everywhere.at[piece_of(e, k), X]
        from_y = everywhere.at[piece_of(e, k), Y]
        links.arrived(from_x, x_id + k)
        if k % 2 == 0:
            links.send(from_x, from_x, d_id + k, seq=Y)
        links.send(from_x, from_x, cx_id + k, seq=C)
        links.arrived(from_y, y_id + k)
        if k % 2:
            links.send(from_y, from_y, d_id + k, seq=X)
        links.send(from_y, from_y, cy_id + k, seq=C)

    def last(k):
        from_d = everywhere.at[piece_of(e, k), D]
        links.arrived(from_d, d_id + k)
        links.send(from_d, from_d, cd_id + k, seq=C)

    def finish(k):
        piece = everywhere.at[piece_of(e, k)]
        links.arrived(piece.at[C], c_id + k)
        links.arrived(piece.at[flipped(C, 2)], cx_id + k)
        links.arrived(piece.at[flipped(C, 4)], cy_id + k)
        links.arrived(piece.at[flipped(flipped(C, 2), 4)], cd_id + k)
        if k == 0:
            local.wait()
        consume(k)

    launch(0)
    for k in range(1, n_exp):
        links.send(own, everywhere.at[e, me], z_id + k, exp=piece_of(e, k))
    for k in range(1, n_exp + 3):
        if k < n_exp:
            launch(k)
        if k - 1 < n_exp:
            relay(k - 1)
        if 0 <= k - 2 < n_exp:
            last(k - 2)
        if 0 <= k - 2 < n_exp:
            finish(k - 2)


def tile_of(size, most=256):
    return next(t for t in range(most, 0, -1) if size % t == 0 and t % 16 == 0)


def times_rows(weights, rows):
    return lax.dot_general(weights, rows, (((1,), (1,)), ((), ())), preferred_element_type=jnp.float32)


def mix_kernel(
    n_seq,
    n_exp,
    part,
    gates,
    gain,
    weights_in,
    rows_out,
    mixed_out,
    gates_out,
    hidden_out,
    by_gate_out,
    by_up_out,
    weights,
    everywhere,
    landed,
    own,
    send_sem,
    recv_sem,
    local_sem,
    rows_sem,
):
    links = Links(send_sem, recv_sem)
    me, e = links.me, links.e
    load = pltpu.make_async_copy(weights_in, weights, local_sem.at[1])
    load.start()
    greet(links, n_exp, True, n_seq)
    r_id, g_id = links.new(n_exp), links.new(n_seq)
    for k in range(1, n_exp):
        links.send(part.at[piece_of(e, k)], landed.at[k - 1], r_id + k, exp=piece_of(e, k))
    for k in range(1, n_seq):
        peer = piece_of(me, k)
        links.send(gates.at[peer], gates_out.at[me], g_id + k, seq=peer)
    gates_out[me] = gates[me]
    total = part[e].astype(jnp.float32)
    for k in range(1, n_exp):
        links.arrived(landed.at[k - 1], r_id + k)
        total = total + landed[k - 1].astype(jnp.float32)
    mixed_out[...] = total
    scale = lax.rsqrt(jnp.mean(total * total, axis=-1, keepdims=True) + EPSILON)
    own[...] = (total * scale * gain[...]).astype(jnp.bfloat16)
    ff, width = weights.shape[1:]
    tile = tile_of(ff)
    stores = []

    def consume(k):
        piece = piece_of(e, k)
        if k == 0:
            load.wait()
        store = pltpu.make_async_copy(everywhere.at[piece], rows_out.at[piece], rows_sem.at[k])
        store.start()
        stores.append(store)

        def step(index, carry):
            at = pl.ds(pl.multiple_of(index * tile, 16), tile)
            rows = everywhere[piece].reshape(-1, width)
            gate_value = times_rows(weights[0, at, :], rows)
            up_value = times_rows(weights[1, at, :], rows)
            squashed = jax.nn.sigmoid(GLU_ALPHA * gate_value)
            glu_value = gate_value * squashed
            hidden_out[piece, at, :] = ((up_value + 1.0) * glu_value).astype(jnp.bfloat16)
            by_gate_out[piece, at, :] = (up_value + 1.0) * (
                squashed + GLU_ALPHA * gate_value * squashed * (1.0 - squashed)
            )
            by_up_out[piece, at, :] = glu_value
            return carry

        lax.fori_loop(0, ff // tile, step, 0)

    spread(links, n_exp, own, everywhere, local_sem.at[0], consume)
    for k in range(1, n_seq):
        links.arrived(gates_out.at[piece_of(me, k)], g_id + k)
    links.drain()
    for store in stores:
        store.wait()


def error_kernel(
    n_seq,
    n_exp,
    hidden,
    gates,
    weights,
    by_gate_in,
    by_up_in,
    mixed,
    control,
    grads_out,
    gate_cols,
    factors,
    everywhere,
    part,
    pair,
    side,
    from_x,
    from_y,
    landed,
    own,
    send_sem,
    recv_sem,
    local_sem,
):
    links = Links(send_sem, recv_sem)
    me, e = links.me, links.e
    core, chip = me % 2, me // 2
    chip_x, chip_y = flipped(chip, 1), flipped(chip, 2)
    chip_d = flipped(chip_x, 2)
    X, Y, C = links.across_x, links.across_y, links.partner
    ff, width = weights.shape
    sub = mixed.shape[0]
    tile = tile_of(ff)
    loads = [
        pltpu.make_async_copy(ref, factors.at[number], local_sem.at[1 + number])
        for number, ref in enumerate((by_gate_in, by_up_in))
    ]
    for load in loads:
        load.start()
    greet(links, n_exp, False, 0)
    p_id, d_id, x_id, y_id, z_id = (links.new(n_exp) for _ in range(5))
    order = list(range(n_exp))[::-1]
    gate_cols[...] = jnp.transpose(jnp.concatenate([gates[number] for number in range(n_seq)], axis=0))

    def gate_col(piece):
        rows = gate_cols[pl.ds(pl.multiple_of(piece * sub, sub), sub), :]
        return jnp.concatenate([rows[:, number : number + 1] for number in range(n_seq)], axis=0)


    def produce(k):
        piece = piece_of(e, k)
        gate = gate_col(piece)
        for start in range(0, width, 512):
            columns = slice(start, min(width, start + 512))
            outs = lax.dot_general(
                hidden[piece], weights[:, columns], (((0,), (0,)), ((), ())), preferred_element_type=jnp.float32
            )
            outs = (outs * gate).astype(jnp.bfloat16)
            part[k, :, :, :, columns] = outs.reshape(n_seq // 2, 2, sub, -1)
        links.send(part.at[k, :, 1 - core], pair.at[k], p_id + k, seq=C)

    def merge(k):
        links.arrived(pair.at[k], p_id + k)
        pair[k] = (pair[k].astype(jnp.float32) + part[k, :, core].astype(jnp.float32)).astype(jnp.bfloat16)
        if k % 2 == 0:
            links.send(pair.at[k, chip_d], side.at[k], d_id + k, seq=X)
            links.send(pair.at[k, chip_x], from_x.at[k], x_id + k, seq=X)
        else:
            links.send(pair.at[k, chip_d], side.at[k], d_id + k, seq=Y)
            links.send(pair.at[k, chip_y], from_y.at[k], y_id + k, seq=Y)

    def pass_on(k):
        links.arrived(side.at[k], d_id + k)
        onward = chip_y if k % 2 == 0 else chip_x
        side[k] = (side[k].astype(jnp.float32) + pair[k, onward].astype(jnp.float32)).astype(jnp.bfloat16)
        if k % 2 == 0:
            links.send(side.at[k], from_y.at[k], y_id + k, seq=Y)
        else:
            links.send(side.at[k], from_x.at[k], x_id + k, seq=X)

    def collect(k):
        links.arrived(from_x.at[k], x_id + k)
        links.arrived(from_y.at[k], y_id + k)
        total = (
            pair[k, chip].astype(jnp.float32)
            + from_x[k].astype(jnp.float32)
            + from_y[k].astype(jnp.float32)
        )
        if k:
            from_x[k] = total.astype(jnp.bfloat16)
            links.send(from_x.at[k], landed.at[k - 1], z_id + k, exp=piece_of(e, k))
        return total

    stages = (produce, merge, pass_on, collect)
    for now in range(n_exp + 3):
        for lag, stage in enumerate(stages):
            if 0 <= now - lag < n_exp and (lag < 3 or now - lag < n_exp - 1):
                stage(order[now - lag])
    steering = control[...]
    target = STEER * steering / jnp.sqrt(jnp.sum(steering * steering, axis=-1, keepdims=True))
    total = collect(0) + mixed[...] - target
    for k in order[:-1]:
        links.arrived(landed.at[k - 1], z_id + k)
        total = total + landed[k - 1].astype(jnp.float32)
    own[...] = total.astype(jnp.bfloat16)
    for load in loads:
        load.wait()

    def consume(k):
        piece = piece_of(e, k)
        gate = jnp.transpose(jnp.broadcast_to(gate_col(piece), (n_seq * sub, 128)))[0:1]
        lanes = pl.ds(pl.multiple_of(piece * (n_seq * sub), n_seq * sub), n_seq * sub)

        def step(index, carry):
            at = pl.ds(pl.multiple_of(index * tile, 16), tile)
            d_hidden = times_rows(weights[at, :], everywhere[piece].reshape(-1, width)) * gate
            grads_out[0, at, lanes] = (d_hidden * factors[0, piece, at, :]).astype(jnp.bfloat16)
            grads_out[1, at, lanes] = (d_hidden * factors[1, piece, at, :]).astype(jnp.bfloat16)
            return carry

        lax.fori_loop(0, ff // tile, step, 0)

    spread(links, n_exp, own, everywhere, local_sem.at[0], consume)
    links.drain()


VM = pl.BlockSpec(memory_space=pltpu.VMEM)
ANY = pl.BlockSpec(memory_space=pl.ANY)


def dense(
    heads_out, out_proj, residual, norm_gain, expert_ids, route_scores, w_gate_up, w_down, control
):
    n_seq, n_exp = lax.axis_size("seq"), lax.axis_size("exp")
    seg_len, width = heads_out.shape[0], out_proj.shape[1]
    sub = seg_len // n_exp
    bf16, f32 = jnp.bfloat16, jnp.float32
    partial_value = jnp.dot(heads_out, out_proj, preferred_element_type=f32)
    column_width = residual.shape[1]
    at = lax.axis_index("exp") * column_width
    placed = lax.dynamic_update_slice_in_dim(jnp.zeros((seg_len, width), bf16), residual, at, 1)
    part = (partial_value + placed.astype(f32)).astype(bf16).reshape(n_exp, sub, width)
    route_gates = route_scores / jnp.sum(route_scores, axis=-1, keepdims=True)
    member = expert_ids[None, :, :] == jnp.arange(n_seq, dtype=jnp.int32)[:, None, None]
    gates = jnp.sum(jnp.where(member, route_gates[None], 0.0), axis=-1).reshape(n_seq, 1, seg_len)
    vectors = jnp.stack([norm_gain, control])
    spread_count = 8 * n_exp
    ff = w_down.shape[1]
    group = n_seq * sub
    rows, mixed, gates_mine, hidden, by_gate, by_up = pl.pallas_call(
        functools.partial(mix_kernel, n_seq, n_exp),
        out_shape=(
            jax.ShapeDtypeStruct((n_exp, n_seq, sub, width), bf16),
            jax.ShapeDtypeStruct((sub, width), f32),
            jax.ShapeDtypeStruct((n_seq, 1, seg_len), f32),
            jax.ShapeDtypeStruct((n_exp, ff, group), bf16),
            jax.ShapeDtypeStruct((n_exp, ff, group), f32),
            jax.ShapeDtypeStruct((n_exp, ff, group), f32),
        ),
        in_specs=[VM, VM, VM, ANY],
        out_specs=(ANY, VM, VM, VM, VM, VM),
        scratch_shapes=[
            pltpu.VMEM((2, ff, width), bf16),
            pltpu.VMEM((n_exp, n_seq, sub, width), bf16),
            pltpu.VMEM((n_exp - 1, sub, width), bf16),
            pltpu.VMEM((sub, width), bf16),
            pltpu.SemaphoreType.DMA((spread_count + n_exp + n_seq,)),
            pltpu.SemaphoreType.DMA((spread_count + n_exp + n_seq,)),
            pltpu.SemaphoreType.DMA((2,)),
            pltpu.SemaphoreType.DMA((n_exp,)),
        ],
        compiler_params=pltpu.CompilerParams(collective_id=0, has_side_effects=True),
        name="mix",
    )(part, gates, vectors[:1], jnp.swapaxes(w_gate_up[0], 1, 2))
    d_both = pl.pallas_call(
        functools.partial(error_kernel, n_seq, n_exp),
        out_shape=jax.ShapeDtypeStruct((2, ff, n_exp * group), bf16),
        in_specs=[VM, VM, VM, ANY, ANY, VM, VM],
        out_specs=VM,
        scratch_shapes=[
            pltpu.VMEM((seg_len, n_seq), f32),
            pltpu.VMEM((2, n_exp, ff, group), f32),
            pltpu.VMEM((n_exp, n_seq, sub, width), bf16),
            pltpu.VMEM((n_exp, n_seq // 2, 2, sub, width), bf16),
            pltpu.VMEM((n_exp, n_seq // 2, sub, width), bf16),
            pltpu.VMEM((n_exp, sub, width), bf16),
            pltpu.VMEM((n_exp, sub, width), bf16),
            pltpu.VMEM((n_exp, sub, width), bf16),
            pltpu.VMEM((n_exp - 1, sub, width), bf16),
            pltpu.VMEM((sub, width), bf16),
            pltpu.SemaphoreType.DMA((spread_count + 5 * n_exp,)),
            pltpu.SemaphoreType.DMA((spread_count + 5 * n_exp,)),
            pltpu.SemaphoreType.DMA((3,)),
        ],
        compiler_params=pltpu.CompilerParams(collective_id=1, has_side_effects=True),
        name="error",
    )(hidden, gates_mine, w_down[0], by_gate, by_up, mixed, vectors[1:])
    grads = lax.dot_general(
        d_both.reshape(2 * ff, n_exp * group),
        rows.reshape(n_exp * group, width),
        (((1,), (0,)), ((), ())),
        preferred_element_type=f32,
    )
    return jnp.swapaxes(grads.astype(bf16).reshape(2, ff, width), 1, 2)[None]


def shards(
    queries,
    attn_keys,
    attn_values,
    sink_logits,
    out_proj,
    residual,
    norm_gain,
    doc_start,
    expert_ids,
    route_scores,
    w_gate_up,
    w_down,
    control,
):
    n_seq = lax.axis_size("seq")
    seg_len = queries.shape[0]
    capacity = 2 * TOPK * seg_len // n_seq
    block_index = lax.axis_index("exp")
    heads_out = attend(queries, attn_keys, attn_values, sink_logits, doc_start)
    if n_seq == 8 and capacity >= seg_len and lax.axis_size("exp") == 4:
        return dense(
            heads_out, out_proj, residual, norm_gain, expert_ids, route_scores, w_gate_up, w_down, control
        )
    partial_value = jnp.dot(heads_out, out_proj, preferred_element_type=jnp.float32)
    column_width = residual.shape[1]
    own_columns = lax.dynamic_slice_in_dim(
        partial_value, block_index * column_width, column_width, 1
    ) + residual.astype(jnp.float32)
    partial_value = lax.dynamic_update_slice_in_dim(
        partial_value, own_columns, block_index * column_width, 1
    )
    mixed = slice_total(partial_value)
    normed = (
        mixed * lax.rsqrt(jnp.mean(mixed * mixed, axis=-1, keepdims=True) + EPSILON) * norm_gain
    ).astype(jnp.bfloat16)
    route_gates = route_scores / jnp.sum(route_scores, axis=-1, keepdims=True)
    flat_ids = expert_ids.reshape(-1)
    onehot = (flat_ids[:, None] == jnp.arange(n_seq, dtype=jnp.int32)[None, :]).astype(jnp.int32)
    slot_rank = jnp.sum((jnp.cumsum(onehot, axis=0) - 1) * onehot, axis=1)
    slot_index = flat_ids * capacity + slot_rank
    owner_row = (
        jnp.zeros((n_seq * capacity,), jnp.int32)
        .at[slot_index]
        .set(jnp.arange(seg_len * TOPK, dtype=jnp.int32))
    )
    filled = (
        jnp.zeros((n_seq * capacity,), jnp.bfloat16)
        .at[slot_index]
        .set(jnp.ones((seg_len * TOPK,), jnp.bfloat16))
    )
    sent_rows = (normed[owner_row // TOPK] * filled[:, None]).reshape(n_seq, capacity, D)
    rows_flat = to_owners(sent_rows).reshape(-1, D)
    gate_slice = w_gate_up[0, 0]
    up_slice = w_gate_up[0, 1]
    down_slice = w_down[0]
    gate_value = jnp.dot(rows_flat, gate_slice, preferred_element_type=jnp.float32)
    up_value = jnp.dot(rows_flat, up_slice, preferred_element_type=jnp.float32)
    squashed = jax.nn.sigmoid(GLU_ALPHA * gate_value)
    glu_value = gate_value * squashed
    hidden = ((up_value + 1.0) * glu_value).astype(jnp.bfloat16)
    out_part = (
        jnp.dot(hidden, down_slice, preferred_element_type=jnp.float32)
        .astype(jnp.bfloat16)
        .reshape(n_seq, capacity, D)
    )
    picked = gather_outputs(out_part, flat_ids, slot_rank, capacity).reshape(seg_len, TOPK, D)
    moe_out = slice_total(jnp.sum(route_gates[:, :, None] * picked, axis=1))
    target = STEER * control / jnp.sqrt(jnp.sum(control * control))
    residual_error = mixed + moe_out - target[None, :]
    d_out = (
        (route_gates[:, :, None] * residual_error[:, None, :])
        .astype(jnp.bfloat16)
        .reshape(seg_len * TOPK, D)
    )
    sent_back = (d_out[owner_row] * filled[:, None]).reshape(n_seq, capacity, D)
    grads_in = to_owners(sent_back).reshape(-1, D)
    d_hidden = lax.dot_general(
        grads_in, down_slice, (((1,), (1,)), ((), ())), preferred_element_type=jnp.float32
    )
    d_gate = (
        d_hidden
        * (up_value + 1.0)
        * (squashed + GLU_ALPHA * gate_value * squashed * (1.0 - squashed))
    ).astype(jnp.bfloat16)
    d_up = (d_hidden * glu_value).astype(jnp.bfloat16)
    grad_gate = lax.dot_general(
        rows_flat, d_gate, (((0,), (0,)), ((), ())), preferred_element_type=jnp.float32
    )
    grad_up = lax.dot_general(
        rows_flat, d_up, (((0,), (0,)), ((), ())), preferred_element_type=jnp.float32
    )
    return jnp.stack([grad_gate, grad_up])[None].astype(jnp.bfloat16)


def solution(mesh):
    return jax.shard_map(
        shards,
        mesh=mesh,
        in_specs=(
            P("seq", "exp"),
            P("seq", "exp"),
            P("seq", "exp"),
            P("exp"),
            P("exp", None),
            P("seq", "exp"),
            P(),
            P("seq"),
            P("seq", None),
            P("seq", None),
            P("seq", None, None, "exp"),
            P("seq", "exp", None),
            P(),
        ),
        out_specs=P("seq", None, None, "exp"),
        check_vma=False,
    )
```

```python
import functools

import jax
import jax.numpy as jnp
from jax import lax
from jax.experimental import pallas as pl
from jax.experimental.pallas import tpu as pltpu
from jax.sharding import PartitionSpec as P

D = 2880
HEAD_DIM = 64
WINDOW = 128
TOPK = 4


GLU_ALPHA = 1.702
STEER = 6.5
EPSILON = 1e-05
MASKED = -1e30
MESH = pl.DeviceIdType.MESH


def passed_along(block, axis, distance):
    devices = range(lax.axis_size(axis))
    route = [(i - distance, i) for i in devices if i - distance in devices]
    return lax.ppermute(block, axis, route)


def attend(queries, attn_keys, attn_values, sink_logits, doc_start):
    seg_len = queries.shape[0]
    heads_here = queries.shape[1] // HEAD_DIM
    kv_here = attn_keys.shape[1] // HEAD_DIM
    group_size = heads_here // kv_here
    both_rims = passed_along(jnp.stack([attn_keys, attn_values]), "seq", 1)
    keys_all = jnp.concatenate([both_rims[0], attn_keys], axis=0).reshape(
        WINDOW + seg_len, kv_here, HEAD_DIM
    )
    values_all = jnp.concatenate([both_rims[1], attn_values], axis=0).reshape(
        WINDOW + seg_len, kv_here, HEAD_DIM
    )
    offset = lax.axis_index("seq") * seg_len
    query_pos = offset + jnp.arange(seg_len, dtype=jnp.int32)
    key_pos = offset - WINDOW + jnp.arange(WINDOW + seg_len, dtype=jnp.int32)
    allowed = (
        (key_pos[None, :] <= query_pos[:, None])
        & (key_pos[None, :] > query_pos[:, None] - WINDOW)
        & (key_pos[None, :] >= doc_start[:, None])
    )
    grouped = queries.reshape(seg_len, kv_here, group_size, HEAD_DIM)
    scores = jnp.einsum(
        "qcgd,kcd->cgqk", grouped, keys_all, preferred_element_type=jnp.float32
    ) * HEAD_DIM ** (-0.5)
    masked_scores = jnp.where(allowed[None, None], scores, MASKED)
    sink_grid = sink_logits.reshape(kv_here, group_size, 1, 1)
    row_top = jnp.maximum(jnp.max(masked_scores, axis=-1, keepdims=True), sink_grid)
    expo_scores = jnp.where(allowed[None, None], jnp.exp(masked_scores - row_top), 0.0)
    denominator = jnp.sum(expo_scores, axis=-1, keepdims=True) + jnp.exp(sink_grid - row_top)
    attn_weights = (expo_scores / denominator).astype(jnp.bfloat16)
    mixed_heads = jnp.einsum(
        "cgqk,kcd->qcgd", attn_weights, values_all, preferred_element_type=jnp.float32
    )
    return mixed_heads.astype(jnp.bfloat16).reshape(seg_len, heads_here * HEAD_DIM)


def slice_total(partial_value):
    return lax.psum(partial_value, "exp")


def to_owners(buffer):
    return lax.all_to_all(buffer, "seq", split_axis=0, concat_axis=0, tiled=True)


def gather_outputs(out_part, flat_ids, slot_rank, capacity):
    width = out_part.shape[-1]
    returned = lax.all_to_all(out_part, "seq", split_axis=0, concat_axis=0, tiled=True).reshape(
        -1, width
    )
    return returned[flat_ids * capacity + slot_rank].astype(jnp.float32)


def flipped(index, bit):
    return index + bit - 2 * bit * ((index // bit) % 2)


class Links:
    def __init__(self, send_sem, recv_sem):
        self.send_sem, self.recv_sem = send_sem, recv_sem
        self.me = lax.axis_index("seq")
        self.e = lax.axis_index("exp")
        self.partner = flipped(self.me, 1)
        self.across_x = flipped(self.me, 2)
        self.across_y = flipped(self.me, 4)
        self.diagonal = flipped(self.across_x, 4)
        self.count = 0
        self.started = []

    def new(self, number=1):
        first = self.count
        self.count += number
        return first

    def copy(self, src, dst, index, seq=None, exp=None):
        device = {"seq": self.me if seq is None else seq, "exp": self.e if exp is None else exp}
        return pltpu.make_async_remote_copy(
            src_ref=src,
            dst_ref=dst,
            send_sem=self.send_sem.at[index],
            recv_sem=self.recv_sem.at[index],
            device_id=device,
            device_id_type=MESH,
        )

    def send(self, src, dst, index, **to):
        sent = self.copy(src, dst, index, **to)
        sent.start()
        self.started.append(sent)

    def arrived(self, dst, index):
        self.copy(dst, dst, index, seq=self.partner).wait_recv()

    def drain(self):
        for sent in self.started:
            sent.wait_send()


def piece_of(e, k):
    out = e
    bit = 1
    while bit <= k:
        if k & bit:
            out = flipped(out, bit)
        bit *= 2
    return out


def greet(links, n_exp, all_seq, n_seq):
    barrier = pltpu.get_barrier_semaphore()
    peers = 0
    flips = range(1, n_seq) if all_seq else [1, 2, 4]
    for k in flips:
        pl.semaphore_signal(
            barrier, inc=1, device_id={"seq": piece_of(links.me, k), "exp": links.e}, device_id_type=MESH
        )
        peers += 1
    for k in range(1, n_exp):
        pl.semaphore_signal(
            barrier, inc=1, device_id={"seq": links.me, "exp": piece_of(links.e, k)}, device_id_type=MESH
        )
        peers += 1
    pl.semaphore_wait(barrier, peers)


def spread(links, n_exp, own, everywhere, local_sem, consume):
    me, e = links.me, links.e
    X, Y, C, D = links.across_x, links.across_y, links.partner, links.diagonal
    z_id, x_id, y_id, c_id = (links.new(n_exp) for _ in range(4))
    d_id, cx_id, cy_id, cd_id = (links.new(n_exp) for _ in range(4))
    local = pltpu.make_async_copy(own, everywhere.at[e, me], local_sem)
    local.start()

    def launch(k):
        spot = everywhere.at[piece_of(e, k), me]
        if k:
            links.arrived(spot, z_id + k)
        src = spot if k else own
        links.send(src, spot, x_id + k, seq=X)
        links.send(src, spot, y_id + k, seq=Y)
        links.send(src, spot, c_id + k, seq=C)

    def relay(k):
        from_x = everywhere.at[piece_of(e, k), X]
        from_y = everywhere.at[piece_of(e, k), Y]
        links.arrived(from_x, x_id + k)
        if k % 2 == 0:
            links.send(from_x, from_x, d_id + k, seq=Y)
        links.send(from_x, from_x, cx_id + k, seq=C)
        links.arrived(from_y, y_id + k)
        if k % 2:
            links.send(from_y, from_y, d_id + k, seq=X)
        links.send(from_y, from_y, cy_id + k, seq=C)

    def last(k):
        from_d = everywhere.at[piece_of(e, k), D]
        links.arrived(from_d, d_id + k)
        links.send(from_d, from_d, cd_id + k, seq=C)

    def finish(k):
        piece = everywhere.at[piece_of(e, k)]
        links.arrived(piece.at[C], c_id + k)
        links.arrived(piece.at[flipped(C, 2)], cx_id + k)
        links.arrived(piece.at[flipped(C, 4)], cy_id + k)
        links.arrived(piece.at[flipped(flipped(C, 2), 4)], cd_id + k)
        if k == 0:
            local.wait()
        consume(k)

    launch(0)
    for k in range(1, n_exp):
        links.send(own, everywhere.at[e, me], z_id + k, exp=piece_of(e, k))
    for k in range(1, n_exp + 3):
        if k < n_exp:
            launch(k)
        if k - 1 < n_exp:
            relay(k - 1)
        if 0 <= k - 2 < n_exp:
            last(k - 2)
        if 0 <= k - 2 < n_exp:
            finish(k - 2)


def tile_of(size, most=256):
    return next(t for t in range(most, 0, -1) if size % t == 0 and t % 16 == 0)


def times_rows(weights, rows):
    return lax.dot_general(weights, rows, (((1,), (1,)), ((), ())), preferred_element_type=jnp.float32)


def mix_kernel(
    n_seq,
    n_exp,
    part,
    expert_ids,
    route_scores,
    gain,
    weights_in,
    rows_out,
    mixed_out,
    gates_out,
    hidden_out,
    by_gate_out,
    by_up_out,
    gates,
    weights,
    everywhere,
    landed,
    own,
    send_sem,
    recv_sem,
    local_sem,
    rows_sem,
):
    links = Links(send_sem, recv_sem)
    me, e = links.me, links.e
    load = pltpu.make_async_copy(weights_in, weights, local_sem.at[1])
    load.start()
    greet(links, n_exp, True, n_seq)
    r_id, g_id = links.new(n_exp), links.new(n_seq)
    for k in range(1, n_exp):
        links.send(part.at[piece_of(e, k)], landed.at[k - 1], r_id + k, exp=piece_of(e, k))
    route_gates = route_scores[...] / jnp.sum(route_scores[...], axis=0, keepdims=True)
    for expert in range(n_seq):
        member = expert_ids[...] == expert
        gates[expert] = jnp.sum(jnp.where(member, route_gates, 0.0), axis=0, keepdims=True)
    for k in range(1, n_seq):
        peer = piece_of(me, k)
        links.send(gates.at[peer], gates_out.at[me], g_id + k, seq=peer)
    gates_out[me] = gates[me]
    total = part[e].astype(jnp.float32)
    for k in range(1, n_exp):
        links.arrived(landed.at[k - 1], r_id + k)
        total = total + landed[k - 1].astype(jnp.float32)
    mixed_out[...] = total
    scale = lax.rsqrt(jnp.mean(total * total, axis=-1, keepdims=True) + EPSILON)
    own[...] = (total * scale * gain[...]).astype(jnp.bfloat16)
    ff, width = weights.shape[1:]
    tile = tile_of(ff)
    stores = []

    def consume(k):
        piece = piece_of(e, k)
        if k == 0:
            load.wait()
        store = pltpu.make_async_copy(everywhere.at[piece], rows_out.at[piece], rows_sem.at[k])
        store.start()
        stores.append(store)

        def step(index, carry):
            at = pl.ds(pl.multiple_of(index * tile, 16), tile)
            rows = everywhere[piece].reshape(-1, width)
            gate_value = times_rows(weights[0, at, :], rows)
            up_value = times_rows(weights[1, at, :], rows)
            squashed = jax.nn.sigmoid(GLU_ALPHA * gate_value)
            glu_value = gate_value * squashed
            hidden_out[piece, at, :] = ((up_value + 1.0) * glu_value).astype(jnp.bfloat16)
            by_gate_out[piece, at, :] = (up_value + 1.0) * (
                squashed + GLU_ALPHA * gate_value * squashed * (1.0 - squashed)
            )
            by_up_out[piece, at, :] = glu_value
            return carry

        lax.fori_loop(0, ff // tile, step, 0)

    spread(links, n_exp, own, everywhere, local_sem.at[0], consume)
    for k in range(1, n_seq):
        links.arrived(gates_out.at[piece_of(me, k)], g_id + k)
    links.drain()
    for store in stores:
        store.wait()


def error_kernel(
    n_seq,
    n_exp,
    hidden,
    gates,
    weights,
    by_gate_in,
    by_up_in,
    mixed,
    control,
    grads_out,
    gate_cols,
    factors,
    everywhere,
    part,
    pair,
    side,
    from_x,
    from_y,
    landed,
    own,
    send_sem,
    recv_sem,
    local_sem,
):
    links = Links(send_sem, recv_sem)
    me, e = links.me, links.e
    core, chip = me % 2, me // 2
    chip_x, chip_y = flipped(chip, 1), flipped(chip, 2)
    chip_d = flipped(chip_x, 2)
    X, Y, C = links.across_x, links.across_y, links.partner
    ff, width = weights.shape
    sub = mixed.shape[0]
    tile = tile_of(ff)
    loads = [
        pltpu.make_async_copy(ref, factors.at[number], local_sem.at[1 + number])
        for number, ref in enumerate((by_gate_in, by_up_in))
    ]
    for load in loads:
        load.start()
    greet(links, n_exp, False, 0)
    p_id, d_id, x_id, y_id, z_id = (links.new(n_exp) for _ in range(5))
    order = list(range(n_exp))[::-1]
    gate_cols[...] = jnp.transpose(jnp.concatenate([gates[number] for number in range(n_seq)], axis=0))

    def gate_col(piece):
        rows = gate_cols[pl.ds(pl.multiple_of(piece * sub, sub), sub), :]
        return jnp.concatenate([rows[:, number : number + 1] for number in range(n_seq)], axis=0)


    def produce(k):
        piece = piece_of(e, k)
        gate = gate_col(piece)
        for start in range(0, width, 512):
            columns = slice(start, min(width, start + 512))
            outs = lax.dot_general(
                hidden[piece], weights[:, columns], (((0,), (0,)), ((), ())), preferred_element_type=jnp.float32
            )
            outs = (outs * gate).astype(jnp.bfloat16)
            part[k, :, :, :, columns] = outs.reshape(n_seq // 2, 2, sub, -1)
        links.send(part.at[k, :, 1 - core], pair.at[k], p_id + k, seq=C)

    def merge(k):
        links.arrived(pair.at[k], p_id + k)
        pair[k] = (pair[k].astype(jnp.float32) + part[k, :, core].astype(jnp.float32)).astype(jnp.bfloat16)
        if k % 2 == 0:
            links.send(pair.at[k, chip_d], side.at[k], d_id + k, seq=X)
            links.send(pair.at[k, chip_x], from_x.at[k], x_id + k, seq=X)
        else:
            links.send(pair.at[k, chip_d], side.at[k], d_id + k, seq=Y)
            links.send(pair.at[k, chip_y], from_y.at[k], y_id + k, seq=Y)

    def pass_on(k):
        links.arrived(side.at[k], d_id + k)
        onward = chip_y if k % 2 == 0 else chip_x
        side[k] = (side[k].astype(jnp.float32) + pair[k, onward].astype(jnp.float32)).astype(jnp.bfloat16)
        if k % 2 == 0:
            links.send(side.at[k], from_y.at[k], y_id + k, seq=Y)
        else:
            links.send(side.at[k], from_x.at[k], x_id + k, seq=X)

    def collect(k):
        links.arrived(from_x.at[k], x_id + k)
        links.arrived(from_y.at[k], y_id + k)
        total = (
            pair[k, chip].astype(jnp.float32)
            + from_x[k].astype(jnp.float32)
            + from_y[k].astype(jnp.float32)
        )
        if k:
            from_x[k] = total.astype(jnp.bfloat16)
            links.send(from_x.at[k], landed.at[k - 1], z_id + k, exp=piece_of(e, k))
        return total

    stages = (produce, merge, pass_on, collect)
    for now in range(n_exp + 3):
        for lag, stage in enumerate(stages):
            if 0 <= now - lag < n_exp and (lag < 3 or now - lag < n_exp - 1):
                stage(order[now - lag])
    steering = control[...]
    target = STEER * steering / jnp.sqrt(jnp.sum(steering * steering, axis=-1, keepdims=True))
    total = collect(0) + mixed[...] - target
    for k in order[:-1]:
        links.arrived(landed.at[k - 1], z_id + k)
        total = total + landed[k - 1].astype(jnp.float32)
    own[...] = total.astype(jnp.bfloat16)
    for load in loads:
        load.wait()

    def consume(k):
        piece = piece_of(e, k)
        gate = jnp.transpose(jnp.broadcast_to(gate_col(piece), (n_seq * sub, 128)))[0:1]
        lanes = pl.ds(pl.multiple_of(piece * (n_seq * sub), n_seq * sub), n_seq * sub)

        def step(index, carry):
            at = pl.ds(pl.multiple_of(index * tile, 16), tile)
            d_hidden = times_rows(weights[at, :], everywhere[piece].reshape(-1, width)) * gate
            grads_out[0, at, lanes] = (d_hidden * factors[0, piece, at, :]).astype(jnp.bfloat16)
            grads_out[1, at, lanes] = (d_hidden * factors[1, piece, at, :]).astype(jnp.bfloat16)
            return carry

        lax.fori_loop(0, ff // tile, step, 0)

    spread(links, n_exp, own, everywhere, local_sem.at[0], consume)
    links.drain()


VM = pl.BlockSpec(memory_space=pltpu.VMEM)
ANY = pl.BlockSpec(memory_space=pl.ANY)


def dense(
    heads_out, out_proj, residual, norm_gain, expert_ids, route_scores, w_gate_up, w_down, control
):
    n_seq, n_exp = lax.axis_size("seq"), lax.axis_size("exp")
    seg_len, width = heads_out.shape[0], out_proj.shape[1]
    sub = seg_len // n_exp
    bf16, f32 = jnp.bfloat16, jnp.float32
    partial_value = jnp.dot(heads_out, out_proj, preferred_element_type=f32)
    column_width = residual.shape[1]
    at = lax.axis_index("exp") * column_width
    placed = lax.dynamic_update_slice_in_dim(jnp.zeros((seg_len, width), bf16), residual, at, 1)
    part = (partial_value + placed.astype(f32)).astype(bf16).reshape(n_exp, sub, width)
    vectors = jnp.stack([norm_gain, control])
    spread_count = 8 * n_exp
    ff = w_down.shape[1]
    group = n_seq * sub
    rows, mixed, gates_mine, hidden, by_gate, by_up = pl.pallas_call(
        functools.partial(mix_kernel, n_seq, n_exp),
        out_shape=(
            jax.ShapeDtypeStruct((n_exp, n_seq, sub, width), bf16),
            jax.ShapeDtypeStruct((sub, width), f32),
            jax.ShapeDtypeStruct((n_seq, 1, seg_len), f32),
            jax.ShapeDtypeStruct((n_exp, ff, group), bf16),
            jax.ShapeDtypeStruct((n_exp, ff, group), f32),
            jax.ShapeDtypeStruct((n_exp, ff, group), f32),
        ),
        in_specs=[VM, VM, VM, VM, ANY],
        out_specs=(ANY, VM, VM, VM, VM, VM),
        scratch_shapes=[
            pltpu.VMEM((n_seq, 1, seg_len), f32),
            pltpu.VMEM((2, ff, width), bf16),
            pltpu.VMEM((n_exp, n_seq, sub, width), bf16),
            pltpu.VMEM((n_exp - 1, sub, width), bf16),
            pltpu.VMEM((sub, width), bf16),
            pltpu.SemaphoreType.DMA((spread_count + n_exp + n_seq,)),
            pltpu.SemaphoreType.DMA((spread_count + n_exp + n_seq,)),
            pltpu.SemaphoreType.DMA((2,)),
            pltpu.SemaphoreType.DMA((n_exp,)),
        ],
        compiler_params=pltpu.CompilerParams(collective_id=0, has_side_effects=True),
        name="mix",
    )(part, expert_ids.T, route_scores.T, vectors[:1], jnp.swapaxes(w_gate_up[0], 1, 2))
    d_both = pl.pallas_call(
        functools.partial(error_kernel, n_seq, n_exp),
        out_shape=jax.ShapeDtypeStruct((2, ff, n_exp * group), bf16),
        in_specs=[VM, VM, VM, ANY, ANY, VM, VM],
        out_specs=VM,
        scratch_shapes=[
            pltpu.VMEM((seg_len, n_seq), f32),
            pltpu.VMEM((2, n_exp, ff, group), f32),
            pltpu.VMEM((n_exp, n_seq, sub, width), bf16),
            pltpu.VMEM((n_exp, n_seq // 2, 2, sub, width), bf16),
            pltpu.VMEM((n_exp, n_seq // 2, sub, width), bf16),
            pltpu.VMEM((n_exp, sub, width), bf16),
            pltpu.VMEM((n_exp, sub, width), bf16),
            pltpu.VMEM((n_exp, sub, width), bf16),
            pltpu.VMEM((n_exp - 1, sub, width), bf16),
            pltpu.VMEM((sub, width), bf16),
            pltpu.SemaphoreType.DMA((spread_count + 5 * n_exp,)),
            pltpu.SemaphoreType.DMA((spread_count + 5 * n_exp,)),
            pltpu.SemaphoreType.DMA((3,)),
        ],
        compiler_params=pltpu.CompilerParams(collective_id=1, has_side_effects=True),
        name="error",
    )(hidden, gates_mine, w_down[0], by_gate, by_up, mixed, vectors[1:])
    grads = lax.dot_general(
        d_both.reshape(2 * ff, n_exp * group),
        rows.reshape(n_exp * group, width),
        (((1,), (0,)), ((), ())),
        preferred_element_type=f32,
    )
    return jnp.swapaxes(grads.astype(bf16).reshape(2, ff, width), 1, 2)[None]


def shards(
    queries,
    attn_keys,
    attn_values,
    sink_logits,
    out_proj,
    residual,
    norm_gain,
    doc_start,
    expert_ids,
    route_scores,
    w_gate_up,
    w_down,
    control,
):
    n_seq = lax.axis_size("seq")
    seg_len = queries.shape[0]
    capacity = 2 * TOPK * seg_len // n_seq
    block_index = lax.axis_index("exp")
    heads_out = attend(queries, attn_keys, attn_values, sink_logits, doc_start)
    if n_seq == 8 and capacity >= seg_len and lax.axis_size("exp") == 4:
        return dense(
            heads_out, out_proj, residual, norm_gain, expert_ids, route_scores, w_gate_up, w_down, control
        )
    partial_value = jnp.dot(heads_out, out_proj, preferred_element_type=jnp.float32)
    column_width = residual.shape[1]
    own_columns = lax.dynamic_slice_in_dim(
        partial_value, block_index * column_width, column_width, 1
    ) + residual.astype(jnp.float32)
    partial_value = lax.dynamic_update_slice_in_dim(
        partial_value, own_columns, block_index * column_width, 1
    )
    mixed = slice_total(partial_value)
    normed = (
        mixed * lax.rsqrt(jnp.mean(mixed * mixed, axis=-1, keepdims=True) + EPSILON) * norm_gain
    ).astype(jnp.bfloat16)
    route_gates = route_scores / jnp.sum(route_scores, axis=-1, keepdims=True)
    flat_ids = expert_ids.reshape(-1)
    onehot = (flat_ids[:, None] == jnp.arange(n_seq, dtype=jnp.int32)[None, :]).astype(jnp.int32)
    slot_rank = jnp.sum((jnp.cumsum(onehot, axis=0) - 1) * onehot, axis=1)
    slot_index = flat_ids * capacity + slot_rank
    owner_row = (
        jnp.zeros((n_seq * capacity,), jnp.int32)
        .at[slot_index]
        .set(jnp.arange(seg_len * TOPK, dtype=jnp.int32))
    )
    filled = (
        jnp.zeros((n_seq * capacity,), jnp.bfloat16)
        .at[slot_index]
        .set(jnp.ones((seg_len * TOPK,), jnp.bfloat16))
    )
    sent_rows = (normed[owner_row // TOPK] * filled[:, None]).reshape(n_seq, capacity, D)
    rows_flat = to_owners(sent_rows).reshape(-1, D)
    gate_slice = w_gate_up[0, 0]
    up_slice = w_gate_up[0, 1]
    down_slice = w_down[0]
    gate_value = jnp.dot(rows_flat, gate_slice, preferred_element_type=jnp.float32)
    up_value = jnp.dot(rows_flat, up_slice, preferred_element_type=jnp.float32)
    squashed = jax.nn.sigmoid(GLU_ALPHA * gate_value)
    glu_value = gate_value * squashed
    hidden = ((up_value + 1.0) * glu_value).astype(jnp.bfloat16)
    out_part = (
        jnp.dot(hidden, down_slice, preferred_element_type=jnp.float32)
        .astype(jnp.bfloat16)
        .reshape(n_seq, capacity, D)
    )
    picked = gather_outputs(out_part, flat_ids, slot_rank, capacity).reshape(seg_len, TOPK, D)
    moe_out = slice_total(jnp.sum(route_gates[:, :, None] * picked, axis=1))
    target = STEER * control / jnp.sqrt(jnp.sum(control * control))
    residual_error = mixed + moe_out - target[None, :]
    d_out = (
        (route_gates[:, :, None] * residual_error[:, None, :])
        .astype(jnp.bfloat16)
        .reshape(seg_len * TOPK, D)
    )
    sent_back = (d_out[owner_row] * filled[:, None]).reshape(n_seq, capacity, D)
    grads_in = to_owners(sent_back).reshape(-1, D)
    d_hidden = lax.dot_general(
        grads_in, down_slice, (((1,), (1,)), ((), ())), preferred_element_type=jnp.float32
    )
    d_gate = (
        d_hidden
        * (up_value + 1.0)
        * (squashed + GLU_ALPHA * gate_value * squashed * (1.0 - squashed))
    ).astype(jnp.bfloat16)
    d_up = (d_hidden * glu_value).astype(jnp.bfloat16)
    grad_gate = lax.dot_general(
        rows_flat, d_gate, (((0,), (0,)), ((), ())), preferred_element_type=jnp.float32
    )
    grad_up = lax.dot_general(
        rows_flat, d_up, (((0,), (0,)), ((), ())), preferred_element_type=jnp.float32
    )
    return jnp.stack([grad_gate, grad_up])[None].astype(jnp.bfloat16)


def solution(mesh):
    return jax.shard_map(
        shards,
        mesh=mesh,
        in_specs=(
            P("seq", "exp"),
            P("seq", "exp"),
            P("seq", "exp"),
            P("exp"),
            P("exp", None),
            P("seq", "exp"),
            P(),
            P("seq"),
            P("seq", None),
            P("seq", None),
            P("seq", None, None, "exp"),
            P("seq", "exp", None),
            P(),
        ),
        out_specs=P("seq", None, None, "exp"),
        check_vma=False,
    )
```
